256 devices in a mesh: mem: 16 (over z_hi, x, core), lev: 16 (over y, z_lo).
Axes of the slice: x: 4, y: 4, z: 8 (z_hi: 2, z_lo: 4; z = z_hi * 4 + z_lo), core: 2. Of those that a mesh axis runs over, the one named last changes fastest.
Arguments:
- alpha_weights: float32 [16, 32, 384, 512], P('mem', 'lev'), may hold values from -6 to 6
- perturbations: bfloat16 [16, 32, 393216], P('mem', None, 'lev'), may hold values from -6 to 6
- coef_x: float32 [384, 512], replicated, may hold values from 0.02 to 0.24
- coef_y: float32 [384, 512], replicated, may hold values from 0.02 to 0.24
- level_scale: float32 [32], replicated, may hold values from 0.3 to 1
- level_map: int32 [32], replicated, may hold values from 0 to 31, each once
- tile_widths: int32 [16], replicated, may hold values from 1 to 24576, 196608 in all
- band_widths: int32 [32], replicated, may hold values from 1 to 4, as said below
Outputs:
- increment: float32 [32, 393216], P('mem', 'lev')
The draws below stay inside these ranges and needn't reach their ends.
Inputs may be any that keep to these rules, and one draw needn't show every extreme that they name: `level_map`: a permutation of the levels. `tile_widths`: sum to 196608; the largest equals 24576. `band_widths`: some level has a band of exactly 4.
All inputs are finite; a program needn't handle non-finite values.
Results may differ from the reference program's by a relative error of at most 0.0035.
Values may be sent and summed in bfloat16 or wider, within the bound.
No kernel may reach another device: no remote copies, remote signals or barrier semaphores. Data moves between devices by JAX's collectives and lax.ppermute only.
A program may use at most 64 MiB of HBM per device.

```python
import math
import jax
import jax.numpy as jnp
import numpy as np
from jax import lax

NX = 384
NY = 512
STEPS = 16
BAND = 4
NLEV = 32
MEMBERS = 16
TILES = 16
CAP = 24576


def draw_band_widths(key, part):
    spot_key, fill_key = jax.random.split(jax.random.fold_in(key, 7))
    widths_drawn = jax.random.randint(fill_key, (NLEV,), 1, BAND + 1)
    marked = jax.random.randint(spot_key, (), 0, NLEV)
    return jnp.where(jnp.arange(NLEV) == marked, BAND, widths_drawn).astype(jnp.int32)


def spiked(entries, stream_key, source, target, blocks, factor):
    def block_of(dim):
        return (jnp.arange(entries.shape[dim]) // (entries.shape[dim] // blocks)).reshape((-1,) + (1,) * (entries.ndim - 1 - dim))

    one_side = jax.random.permutation(stream_key, blocks)[block_of(target)]
    far = (block_of(target) + blocks // 2) % blocks
    return jnp.where((block_of(source) == one_side) | (block_of(source) == far), factor * entries, entries)


def level_of(key, extent, pieces, low, largest):
    def one(axis_at, shards_of):
        heights = jax.random.uniform(jax.random.fold_in(jax.random.fold_in(key, 6), axis_at), (shards_of,), jnp.float32, low / len(pieces), largest / len(pieces))
        return jnp.repeat(jnp.exp(heights), extent[axis_at] // shards_of).reshape((-1,) + (1,) * (len(extent) - axis_at - 1))

    level = one(*pieces[0])
    for cut in pieces[1:]:
        level = level * one(*cut)
    return level


def length_profile(number_of, total, reach, skew):
    loads = [(1 << 20) // math.isqrt(grade ** skew) + 1 for grade in range(2, number_of + 1)]
    spare, holding = total - reach - (number_of - 1), [1] * (number_of - 1)
    while spare > 0:
        candidates = [i for i in range(number_of - 1) if holding[i] < reach]
        pool, left = sum([loads[i] for i in candidates]), spare
        for i in candidates:
            extra = min(reach - holding[i], max(1, left * loads[i] // pool), spare)
            holding[i] = holding[i] + extra
            spare = spare - extra
    return np.array([reach] + holding)


def ragged_sizes(stream_key, number_of, total, limit, skew):
    if number_of == 2:
        one = jax.random.randint(stream_key, (), max(1, total - limit), min(limit, total - 1) + 1)
        return jnp.stack([one, total - one])
    sizes = jnp.asarray(length_profile(number_of, total, limit, skew), jnp.int32)
    twos = (number_of - 1) // 2
    donor, taker = sizes[1:1 + 2 * twos:2], sizes[2:2 + 2 * twos:2]
    slack = jnp.minimum(donor - 1, limit - taker)
    moved = jax.random.randint(jax.random.fold_in(stream_key, 1), (twos,), 0, 1 << 20) % (slack + 1)
    sizes = sizes.at[1:1 + 2 * twos:2].set(donor - moved).at[2:2 + 2 * twos:2].set(taker + moved)
    return sizes[jax.random.permutation(jax.random.fold_in(stream_key, 2), number_of)]


def bell_draw(stream_key, shape, width, most, cuts=(), kind=jnp.bfloat16):
    result = jax.random.normal(stream_key, shape, jnp.float32) * width
    if len(cuts) > 0:
        result = level_of(stream_key, shape, cuts, -0.22, 0.18) * result
    return jnp.clip(result, min=-most, max=most).astype(kind)


def bell_draw_with(stream_key, dims, scale, most, shards, heavy, kind=jnp.bfloat16):
    array = scale * jax.random.normal(stream_key, dims, jnp.float32)
    if shards:
        array = array * level_of(stream_key, dims, shards, -0.22, 0.18)
    return jnp.clip(spiked(array, jax.random.fold_in(stream_key, 3), *heavy), -most, most).astype(kind)


def setup_inputs(seed: int = 0) -> dict:
    keys = jax.random.split(jax.random.key(seed), 9)
    return {
        "alpha_weights": bell_draw(keys[0], (MEMBERS, NLEV, NX, NY), 1.0, 6.0, ((0, 16), (1, 16)), jnp.float32),
        "perturbations": bell_draw_with(keys[1], (MEMBERS, NLEV, TILES * CAP), 1.0, 6.0, ((0, 16), (2, 16)), (0, 1, 16, 2.0)),
        "coef_x": jnp.clip(jax.random.uniform(keys[2], (NX, NY), jnp.float32, 0.02, 0.24), 0.02, 0.24),
        "coef_y": jnp.clip(jax.random.uniform(keys[3], (NX, NY), jnp.float32, 0.02, 0.24), 0.02, 0.24),
        "level_scale": jnp.clip(jnp.exp(jax.random.uniform(keys[4], (NLEV,), jnp.float32, math.log(0.3), math.log(1.0))), 0.3, 1.0),
        "level_map": jax.random.permutation(keys[5], NLEV).astype(jnp.int32),
        "tile_widths": ragged_sizes(keys[6], TILES, NX * NY, CAP, 2).astype(jnp.int32),
        "band_widths": draw_band_widths(jax.random.fold_in(keys[8], 71), 0),
    }


def diffuse_level(layer_field, scaled_x, scaled_y):
    def step_once(index_step, state):
        flux_x = scaled_x[:-1, :] * (state[1:, :] - state[:-1, :])
        flux_y = scaled_y[:, :-1] * (state[:, 1:] - state[:, :-1])
        zero_row = jnp.zeros((1, state.shape[1]), state.dtype)
        zero_col = jnp.zeros((state.shape[0], 1), state.dtype)
        change = jnp.concatenate([flux_x, zero_row], 0) - jnp.concatenate([zero_row, flux_x], 0)
        change = change + jnp.concatenate([flux_y, zero_col], 1) - jnp.concatenate([zero_col, flux_y], 1)
        return state + change
    return lax.fori_loop(0, STEPS, step_once, layer_field)


def vertical_matrix(band_widths):
    level_pos = jnp.arange(band_widths.shape[0])
    distance = jnp.abs(level_pos[:, None] - level_pos[None, :]).astype(jnp.float32)
    mutual = jnp.minimum(band_widths[:, None], band_widths[None, :]).astype(jnp.float32)
    return jnp.where(distance <= mutual, jnp.exp(-distance * distance / (mutual * mutual)), 0.0)


def reference(alpha_weights, perturbations, coef_x, coef_y, level_scale, level_map, tile_widths, band_widths):
    starts = jnp.cumsum(tile_widths) - tile_widths
    slot_pos = jnp.arange(TILES * CAP)
    tile_id = slot_pos // CAP
    offset = slot_pos % CAP
    valid_cols = offset < tile_widths[tile_id]
    column = jnp.minimum(starts[tile_id] + offset, NX * NY - 1).astype(jnp.int32)
    localizer = vertical_matrix(band_widths).astype(jnp.bfloat16)
    slot_scale = level_scale[level_map]

    def smooth_slot(member_field, strength):
        return diffuse_level(member_field, coef_x * strength, coef_y * strength)

    def member(running, member_pair):
        member_field, pert_rows = member_pair
        smooth = jax.vmap(smooth_slot)(member_field, slot_scale)
        rounded = smooth.astype(jnp.bfloat16).reshape(NLEV, NX * NY)
        physical = jnp.zeros_like(rounded).at[level_map].set(rounded)
        tiled_cols = physical[:, column]
        spread = jnp.dot(localizer, tiled_cols, preferred_element_type=jnp.float32)
        return running + jnp.where(valid_cols[None, :], pert_rows.astype(jnp.float32) * spread, 0.0), None

    running, unused = lax.scan(member, jnp.zeros((NLEV, TILES * CAP), jnp.float32), (alpha_weights, perturbations))
    return running
```

```python
import jax
import jax.numpy as jnp
from jax import lax
from jax.experimental import pallas as pl
from jax.experimental.pallas import tpu as pltpu
from jax.sharding import PartitionSpec as P

STEPS = 16
LANES = 128
SUBS = 8
ROWS_PER_BLOCK = 8
CORES, RING, HALVES = 2, 4, 2


def split_bf16(x):
    high = x.astype(jnp.bfloat16)
    return high, (x - high.astype(jnp.float32)).astype(jnp.bfloat16)


def diffuse_kernel(
    place_ref, scale_ref, map_ref, width_ref, alpha_ref, cx_ref, cy_ref, spread_ref, gather_ref,
    out_ref, raw_scr, cx_scr, cy_scr, x_scr, f_scr, gx_scr, gy_scr, ax_scr, ay_scr, ayr_scr, o_scr,
    msg_scr, sems, out_sem,
):
    rows, cols = cx_ref.shape
    levels = alpha_ref.shape[1]
    fold = rows // SUBS
    blocks = cols // LANES
    tiles, _, length = out_ref.shape

    def part(b):
        return pl.ds(b * LANES, LANES)

    copies = []
    for b in range(blocks):
        one = [
            pltpu.make_async_copy(cx_ref.at[:, part(b)], cx_scr.at[b], sems.at[b, 0]),
            pltpu.make_async_copy(cy_ref.at[:, part(b)], cy_scr.at[b], sems.at[b, 1]),
        ]
        for v in range(levels):
            one.append(
                pltpu.make_async_copy(
                    alpha_ref.at[0, v, :, part(b)], raw_scr.at[v, b], sems.at[b, 2 + v]
                )
            )
        copies.append(one)
    for k in range(2 + levels):
        for b in range(blocks):
            copies[b][k].start()

    def spread_columns(planes):
        for r in range(fold):
            for b in range(blocks):
                x_scr[pl.ds(r * SUBS, SUBS), part(b)] = planes[b, pl.ds(r, SUBS, stride=fold), :]
        high, low = split_bf16(x_scr[...])
        return jnp.dot(high, spread_ref[...], preferred_element_type=jnp.float32) + jnp.dot(
            low, spread_ref[...], preferred_element_type=jnp.float32
        )

    lane = lax.broadcasted_iota(jnp.int32, (SUBS, LANES), 1)
    sub = lax.broadcasted_iota(jnp.int32, (SUBS, LANES), 0)
    for b in range(blocks):
        copies[b][0].wait()
    gx_scr[...] = spread_columns(cx_scr)
    for b in range(blocks):
        copies[b][1].wait()
    gy_scr[...] = spread_columns(cy_scr)

    def at(r):
        return pl.ds(r * SUBS, SUBS)

    for v in range(levels):
        gain = scale_ref[map_ref[place_ref[0] * levels + v]]
        for b in range(blocks):
            copies[b][2 + v].wait()
        f_scr[pl.ds(0, rows), :] = spread_columns(raw_scr.at[v])
        for r in range(fold):
            for b in range(blocks):
                ax = gx_scr[at(r), part(b)] * gain
                ay = gy_scr[at(r), part(b)] * gain
                if r == fold - 1:
                    ax = jnp.where(sub == SUBS - 1, 0.0, ax)
                if b == blocks - 1:
                    ay = jnp.where(lane == LANES - 1, 0.0, ay)
                    ayr_scr[at(r), :] = pltpu.roll(ay, 1, 1)
                ax_scr[at(r), part(b)] = ax
                ay_scr[at(r), part(b)] = ay

        @pl.loop(0, STEPS)
        def _(step):
            wrap = [pltpu.roll(f_scr[at(0), part(b)], SUBS - 1, 0) for b in range(blocks)]
            for b in range(blocks):
                f_scr[at(fold), part(b)] = wrap[b]
            here = [f_scr[at(fold - 1), part(b)] for b in range(blocks)]
            before = [
                pltpu.roll(ax_scr[at(fold - 1), part(b)] * (wrap[b] - here[b]), 1, 0)
                for b in range(blocks)
            ]
            here = [f_scr[at(0), part(b)] for b in range(blocks)]
            for r in range(fold):
                after = [f_scr[at(r + 1), part(b)] for b in range(blocks)]
                right = pltpu.roll(here[0], LANES - 1, 1)
                left = pltpu.roll(here[blocks - 1], 1, 1)
                last_y = ayr_scr[at(r), :] * (here[0] - left)
                flux = []
                for b in range(blocks):
                    fx = ax_scr[at(r), part(b)] * (after[b] - here[b])
                    beside = here[b + 1] if b < blocks - 1 else right
                    fy = ay_scr[at(r), part(b)] * (beside - here[b])
                    f_scr[at(r), part(b)] = here[b] + (fx - before[b]) + (fy - last_y)
                    last_y = fy
                    flux.append(fx)
                here, before = after, flux

        x_scr[...] = jnp.dot(
            f_scr[pl.ds(0, rows), :].astype(jnp.bfloat16),
            gather_ref[...],
            preferred_element_type=jnp.float32,
        )
        for r in range(fold):
            for b in range(blocks):
                o_scr[pl.ds(r * SUBS + b * levels + v, SUBS, stride=rows), :] = x_scr[at(r), part(b)]

    for i in range(rows):
        msg_scr[:, part(i)] = o_scr[at(i), :].astype(jnp.bfloat16)
    spare = msg_scr.shape[1] - rows * LANES
    msg_scr[:, pl.ds(rows * LANES, spare)] = jnp.zeros((SUBS, spare), jnp.bfloat16)
    first_col = 0
    sends = []
    for t in range(tiles):
        first = pl.multiple_of(first_col // cols * LANES, LANES)
        sends.append(
            pltpu.make_async_copy(
                msg_scr.at[:, pl.ds(first, length)], out_ref.at[t], out_sem.at[t]
            )
        )
        sends[-1].start()
        first_col = first_col + width_ref[t]
    for one in sends:
        one.wait()


def smooth_and_cut(place, level_scale, level_map, tile_widths, alpha, coef_x, coef_y, capacity):
    _, levels, rows, cols = alpha.shape
    tiles = tile_widths.shape[0]
    blocks = cols // LANES
    assert levels * blocks == SUBS and rows % SUBS == 0
    tile_rows = pl.cdiv(capacity, cols) + 1
    length = tile_rows * LANES
    natural = lax.broadcasted_iota(jnp.int32, (cols, cols), 0)
    spaced = lax.broadcasted_iota(jnp.int32, (cols, cols), 1)
    spread = (natural == spaced % LANES * blocks + spaced // LANES).astype(jnp.bfloat16)
    anywhere = pl.BlockSpec(memory_space=pl.ANY)
    scalars = pl.BlockSpec(memory_space=pltpu.SMEM)
    vector = pl.BlockSpec(memory_space=pltpu.VMEM)
    plane = pltpu.VMEM((blocks, rows, LANES), jnp.float32)
    whole = pltpu.VMEM((rows, cols), jnp.float32)
    return pl.pallas_call(
        diffuse_kernel,
        out_shape=jax.ShapeDtypeStruct((tiles, SUBS, length), jnp.bfloat16),
        in_specs=[scalars] * 4 + [anywhere] * 3 + [vector] * 2,
        out_specs=anywhere,
        scratch_shapes=[
            pltpu.VMEM((levels, blocks, rows, LANES), jnp.float32),
            plane,
            plane,
            whole,
            pltpu.VMEM((rows + SUBS, cols), jnp.float32),
            whole,
            whole,
            whole,
            whole,
            pltpu.VMEM((rows, LANES), jnp.float32),
            pltpu.VMEM((rows * SUBS, LANES), jnp.float32),
            pltpu.VMEM((SUBS, (rows + tile_rows) * LANES), jnp.bfloat16),
            pltpu.SemaphoreType.DMA((blocks, 2 + levels)),
            pltpu.SemaphoreType.DMA((tiles,)),
        ],
        name="diffuse",
    )(place, level_scale, level_map, tile_widths, alpha, coef_x, coef_y, spread, spread.T)


def localize_kernel(place_ref, width_ref, x_ref, weight_ref, order_ref, pert_ref, own_ref, send_ref, s_scr):
    step = pl.program_id(0)
    tiles = width_ref.shape[0]
    levels = order_ref.shape[0]
    blocks = weight_ref.shape[0] // levels
    cols = blocks * LANES
    chunk = pert_ref.shape[2]
    count = chunk // cols
    me = place_ref[0]
    first_col = 0
    for t in range(tiles):
        first_col = first_col + jnp.where(t < me, width_ref[t], 0)
    shift = first_col % cols
    shift_blocks = shift // LANES
    shift_lanes = shift % LANES
    width = width_ref[me] - step * chunk
    begin = pl.multiple_of(step * (count * LANES), LANES)
    spread = jnp.dot(
        weight_ref[...],
        x_ref[:, pl.ds(begin, (count + 1) * LANES)],
        preferred_element_type=jnp.float32,
    )
    for r in range(count + 1):
        for b in range(blocks):
            s_scr[:, pl.ds((r * blocks + b) * LANES, LANES)] = spread[
                b * levels : (b + 1) * levels, r * LANES : (r + 1) * LANES
            ]
    ordered = jnp.dot(order_ref[...], pert_ref[0], preferred_element_type=jnp.float32)
    lane = lax.broadcasted_iota(jnp.int32, (levels, LANES), 1)
    keep = lane < LANES - shift_lanes
    half = levels // 2

    def rolled(k):
        block = s_scr[:, pl.ds(pl.multiple_of((k + shift_blocks) * LANES, LANES), LANES)]
        return pltpu.roll(block, lax.rem(LANES - shift_lanes, LANES), 1)

    here = rolled(0)
    for k in range(count * blocks):
        after = rolled(k + 1)
        at = jnp.where(keep, here, after)
        part = pl.ds(k * LANES, LANES)
        value = ordered[:, k * LANES : (k + 1) * LANES] * at
        value = jnp.where(lane < width - k * LANES, value, 0.0).astype(jnp.bfloat16)
        own_ref[:, part] = value[:half]
        send_ref[:, part] = value[half:]
        here = after


def localize(place, tile_widths, arrived, weight, order, perturbations):
    _, levels, capacity = perturbations.shape
    blocks = weight.shape[0] // levels
    cols = blocks * LANES
    chunk = ROWS_PER_BLOCK * cols
    assert capacity % chunk == 0
    scalars = pl.BlockSpec(memory_space=pltpu.SMEM)
    vector = pl.BlockSpec(memory_space=pltpu.VMEM)
    half = jax.ShapeDtypeStruct((levels // 2, capacity), jnp.bfloat16)
    half_spec = pl.BlockSpec((levels // 2, chunk), lambda i: (0, i))
    return pl.pallas_call(
        localize_kernel,
        grid=(capacity // chunk,),
        out_shape=(half, half),
        in_specs=[scalars, scalars, vector, vector, vector,
                  pl.BlockSpec((1, levels, chunk), lambda i: (0, 0, i))],
        out_specs=(half_spec, half_spec),
        scratch_shapes=[pltpu.VMEM((levels, chunk + 2 * cols), jnp.float32)],
        name="localize",
    )(place, tile_widths, arrived, weight, order, perturbations)


def body(
    alpha_weights, perturbations, coef_x, coef_y, level_scale, level_map, tile_widths, band_widths
):
    _, lev_dev, rows, cols = alpha_weights.shape
    _, levels, capacity = perturbations.shape
    blocks = cols // LANES
    tiles = tile_widths.shape[0]
    mem = lax.axis_index("mem")
    place = lax.axis_index("lev").astype(jnp.int32).reshape(1)

    outgoing = smooth_and_cut(
        place, level_scale, level_map, tile_widths, alpha_weights, coef_x, coef_y, capacity
    )
    arrived = lax.all_to_all(outgoing, "lev", split_axis=0, concat_axis=0, tiled=True)
    arrived = arrived.reshape(tiles * SUBS, -1)

    slot = jnp.arange(levels)
    core = (mem + slot // 16) % CORES
    ring = (mem // CORES + slot // 4) % RING
    half = (mem // (CORES * RING) + slot // 2) % HALVES
    row_level = half * 16 + ring * 4 + core * 2 + slot % 2
    order = (row_level[:, None] == slot[None, :]).astype(jnp.bfloat16)
    row_band = jnp.sum(jnp.where(row_level[:, None] == slot[None, :], band_widths[None, :], 0), 1)
    col_band = jnp.sum(jnp.where(level_map[:, None] == slot[None, :], band_widths[None, :], 0), 1)
    distance = jnp.abs(row_level[:, None] - level_map[None, :]).astype(jnp.float32)
    mutual = jnp.minimum(row_band[:, None], col_band[None, :]).astype(jnp.float32)
    local = jnp.where(distance <= mutual, jnp.exp(-distance * distance / (mutual * mutual)), 0.0)
    same_block = (jnp.arange(blocks)[:, None] == jnp.arange(blocks)[None, :])[:, None, None, :, None]
    weight = jnp.where(same_block, local.reshape(1, levels, tiles, 1, lev_dev), 0.0)
    weight = weight.astype(jnp.bfloat16).reshape(blocks * levels, tiles * SUBS)

    own, other = localize(place, tile_widths, arrived, weight, order, perturbations)

    def wide(x):
        return x.astype(jnp.float32)

    members = CORES * RING * HALVES
    came = lax.ppermute(other, "mem", [(i, i ^ 1) for i in range(members)])
    pair = (wide(own) + wide(came)).astype(jnp.bfloat16).reshape(RING, 4, capacity)
    total = wide(pair[0])
    for d in range(1, RING):
        ring_perm = [
            (z * 8 + x * 2 + c, z * 8 + (x + d) % RING * 2 + c)
            for z in range(HALVES)
            for x in range(RING)
            for c in range(CORES)
        ]
        total = total + wide(lax.ppermute(pair[d], "mem", ring_perm))
    came = lax.ppermute(
        total[2:].astype(jnp.bfloat16), "mem", [(i, (i + 8) % members) for i in range(members)]
    )
    return total[:2] + wide(came)


def solution(mesh):
    placed = (P("mem", "lev", None, None), P("mem", None, "lev"), P(), P(), P(), P(), P(), P())
    return jax.shard_map(
        body, mesh=mesh, in_specs=placed, out_specs=P("mem", "lev"), check_vma=False
    )
```

```python
import functools

import jax
import jax.numpy as jnp
from jax import lax
from jax.experimental import pallas as pl
from jax.experimental.pallas import tpu as pltpu
from jax.sharding import PartitionSpec as P

STEPS = 16
LANES = 128
SUBS = 8
ROWS_PER_BLOCK = 8
PIECES = (24, 24)
CORES, RING, HALVES = 2, 4, 2


def split_bf16(x):
    high = x.astype(jnp.bfloat16)
    return high, (x - high.astype(jnp.float32)).astype(jnp.bfloat16)


def diffuse_kernel(
    place_ref, scale_ref, map_ref, width_ref, alpha_ref, cx_ref, cy_ref, spread_ref, gather_ref,
    *refs,
):
    out_refs = refs[: len(PIECES)]
    (
        raw_scr, cx_scr, cy_scr, x_scr, f_scr, gx_scr, gy_scr, ax_scr, ay_scr, ayr_scr, o_scr,
        msg_scr, sems, out_sem,
    ) = refs[len(PIECES) :]
    rows, cols = cx_ref.shape
    levels = alpha_ref.shape[1]
    fold = rows // SUBS
    blocks = cols // LANES
    tiles = width_ref.shape[0]

    def part(b):
        return pl.ds(b * LANES, LANES)

    copies = []
    for b in range(blocks):
        one = [
            pltpu.make_async_copy(cx_ref.at[:, part(b)], cx_scr.at[b], sems.at[b, 0]),
            pltpu.make_async_copy(cy_ref.at[:, part(b)], cy_scr.at[b], sems.at[b, 1]),
        ]
        for v in range(levels):
            one.append(
                pltpu.make_async_copy(
                    alpha_ref.at[0, v, :, part(b)], raw_scr.at[v, b], sems.at[b, 2 + v]
                )
            )
        copies.append(one)
    for k in range(2 + levels):
        for b in range(blocks):
            copies[b][k].start()

    def spread_columns(planes):
        for r in range(fold):
            for b in range(blocks):
                x_scr[pl.ds(r * SUBS, SUBS), part(b)] = planes[b, pl.ds(r, SUBS, stride=fold), :]
        high, low = split_bf16(x_scr[...])
        return jnp.dot(high, spread_ref[...], preferred_element_type=jnp.float32) + jnp.dot(
            low, spread_ref[...], preferred_element_type=jnp.float32
        )

    lane = lax.broadcasted_iota(jnp.int32, (SUBS, LANES), 1)
    sub = lax.broadcasted_iota(jnp.int32, (SUBS, LANES), 0)
    for b in range(blocks):
        copies[b][0].wait()
    gx_scr[...] = spread_columns(cx_scr)
    for b in range(blocks):
        copies[b][1].wait()
    gy_scr[...] = spread_columns(cy_scr)

    def at(r):
        return pl.ds(r * SUBS, SUBS)

    for v in range(levels):
        gain = scale_ref[map_ref[place_ref[0] * levels + v]]
        for b in range(blocks):
            copies[b][2 + v].wait()
        f_scr[pl.ds(0, rows), :] = spread_columns(raw_scr.at[v])
        for r in range(fold):
            for b in range(blocks):
                ax = gx_scr[at(r), part(b)] * gain
                ay = gy_scr[at(r), part(b)] * gain
                if r == fold - 1:
                    ax = jnp.where(sub == SUBS - 1, 0.0, ax)
                if b == blocks - 1:
                    ay = jnp.where(lane == LANES - 1, 0.0, ay)
                    ayr_scr[at(r), :] = pltpu.roll(ay, 1, 1)
                ax_scr[at(r), part(b)] = ax
                ay_scr[at(r), part(b)] = ay

        @pl.loop(0, STEPS)
        def _(step):
            wrap = [pltpu.roll(f_scr[at(0), part(b)], SUBS - 1, 0) for b in range(blocks)]
            for b in range(blocks):
                f_scr[at(fold), part(b)] = wrap[b]
            here = [f_scr[at(fold - 1), part(b)] for b in range(blocks)]
            before = [
                pltpu.roll(ax_scr[at(fold - 1), part(b)] * (wrap[b] - here[b]), 1, 0)
                for b in range(blocks)
            ]
            here = [f_scr[at(0), part(b)] for b in range(blocks)]
            for r in range(fold):
                after = [f_scr[at(r + 1), part(b)] for b in range(blocks)]
                right = pltpu.roll(here[0], LANES - 1, 1)
                left = pltpu.roll(here[blocks - 1], 1, 1)
                last_y = ayr_scr[at(r), :] * (here[0] - left)
                flux = []
                for b in range(blocks):
                    fx = ax_scr[at(r), part(b)] * (after[b] - here[b])
                    beside = here[b + 1] if b < blocks - 1 else right
                    fy = ay_scr[at(r), part(b)] * (beside - here[b])
                    f_scr[at(r), part(b)] = here[b] + (fx - before[b]) + (fy - last_y)
                    last_y = fy
                    flux.append(fx)
                here, before = after, flux

        x_scr[...] = jnp.dot(
            f_scr[pl.ds(0, rows), :].astype(jnp.bfloat16),
            gather_ref[...],
            preferred_element_type=jnp.float32,
        )
        for r in range(fold):
            for b in range(blocks):
                o_scr[pl.ds(r * SUBS + b * levels + v, SUBS, stride=rows), :] = x_scr[at(r), part(b)]

    for i in range(rows):
        msg_scr[:, part(i)] = o_scr[at(i), :].astype(jnp.bfloat16)
    spare = msg_scr.shape[1] - rows * LANES
    msg_scr[:, pl.ds(rows * LANES, spare)] = jnp.zeros((SUBS, spare), jnp.bfloat16)
    sends = []
    begin = 0
    for p, out_ref in enumerate(out_refs):
        first_col = 0
        for t in range(tiles):
            first = pl.multiple_of((first_col // cols + begin) * LANES, LANES)
            sends.append(
                pltpu.make_async_copy(
                    msg_scr.at[:, pl.ds(first, out_ref.shape[2])], out_ref.at[t], out_sem.at[p, t]
                )
            )
            sends[-1].start()
            first_col = first_col + width_ref[t]
        begin += PIECES[p]
    for one in sends:
        one.wait()


def smooth_and_cut(place, level_scale, level_map, tile_widths, alpha, coef_x, coef_y, capacity):
    _, levels, rows, cols = alpha.shape
    tiles = tile_widths.shape[0]
    blocks = cols // LANES
    assert levels * blocks == SUBS and rows % SUBS == 0
    tile_rows = capacity // cols + 1
    assert sum(PIECES) == tile_rows - 1
    natural = lax.broadcasted_iota(jnp.int32, (cols, cols), 0)
    spaced = lax.broadcasted_iota(jnp.int32, (cols, cols), 1)
    spread = (natural == spaced % LANES * blocks + spaced // LANES).astype(jnp.bfloat16)
    anywhere = pl.BlockSpec(memory_space=pl.ANY)
    scalars = pl.BlockSpec(memory_space=pltpu.SMEM)
    vector = pl.BlockSpec(memory_space=pltpu.VMEM)
    plane = pltpu.VMEM((blocks, rows, LANES), jnp.float32)
    whole = pltpu.VMEM((rows, cols), jnp.float32)
    return pl.pallas_call(
        diffuse_kernel,
        out_shape=[
            jax.ShapeDtypeStruct((tiles, SUBS, (n + 1) * LANES), jnp.bfloat16) for n in PIECES
        ],
        in_specs=[scalars] * 4 + [anywhere] * 3 + [vector] * 2,
        out_specs=[anywhere] * len(PIECES),
        scratch_shapes=[
            pltpu.VMEM((levels, blocks, rows, LANES), jnp.float32),
            plane,
            plane,
            whole,
            pltpu.VMEM((rows + SUBS, cols), jnp.float32),
            whole,
            whole,
            whole,
            whole,
            pltpu.VMEM((rows, LANES), jnp.float32),
            pltpu.VMEM((rows * SUBS, LANES), jnp.float32),
            pltpu.VMEM((SUBS, (rows + tile_rows) * LANES), jnp.bfloat16),
            pltpu.SemaphoreType.DMA((blocks, 2 + levels)),
            pltpu.SemaphoreType.DMA((len(PIECES), tiles)),
        ],
        name="diffuse",
    )(place, level_scale, level_map, tile_widths, alpha, coef_x, coef_y, spread, spread.T)


def localize_kernel(
    begin_row, place_ref, width_ref, x_ref, weight_ref, order_ref, pert_ref, own_ref, send_ref, s_scr
):
    step = pl.program_id(0)
    tiles = width_ref.shape[0]
    levels = order_ref.shape[0]
    blocks = weight_ref.shape[0] // levels
    cols = blocks * LANES
    chunk = pert_ref.shape[2]
    count = chunk // cols
    me = place_ref[0]
    first_col = 0
    for t in range(tiles):
        first_col = first_col + jnp.where(t < me, width_ref[t], 0)
    shift = first_col % cols
    shift_blocks = shift // LANES
    shift_lanes = shift % LANES
    width = width_ref[me] - begin_row * cols - step * chunk
    begin = pl.multiple_of(step * (count * LANES), LANES)
    spread = jnp.dot(
        weight_ref[...],
        x_ref[:, pl.ds(begin, (count + 1) * LANES)],
        preferred_element_type=jnp.float32,
    )
    for r in range(count + 1):
        for b in range(blocks):
            s_scr[:, pl.ds((r * blocks + b) * LANES, LANES)] = spread[
                b * levels : (b + 1) * levels, r * LANES : (r + 1) * LANES
            ]
    ordered = jnp.dot(order_ref[...], pert_ref[0], preferred_element_type=jnp.float32)
    lane = lax.broadcasted_iota(jnp.int32, (levels, LANES), 1)
    keep = lane < LANES - shift_lanes
    half = levels // 2

    def rolled(k):
        block = s_scr[:, pl.ds(pl.multiple_of((k + shift_blocks) * LANES, LANES), LANES)]
        return pltpu.roll(block, lax.rem(LANES - shift_lanes, LANES), 1)

    here = rolled(0)
    for k in range(count * blocks):
        after = rolled(k + 1)
        at = jnp.where(keep, here, after)
        part = pl.ds(k * LANES, LANES)
        value = ordered[:, k * LANES : (k + 1) * LANES] * at
        value = jnp.where(lane < width - k * LANES, value, 0.0).astype(jnp.bfloat16)
        own_ref[:, part] = value[:half]
        send_ref[:, part] = value[half:]
        here = after


def localize(begin_row, rows, place, tile_widths, arrived, weight, order, perturbations):
    levels = perturbations.shape[1]
    blocks = weight.shape[0] // levels
    cols = blocks * LANES
    chunk = ROWS_PER_BLOCK * cols
    assert rows % ROWS_PER_BLOCK == 0 and begin_row % ROWS_PER_BLOCK == 0
    skip = begin_row // ROWS_PER_BLOCK
    scalars = pl.BlockSpec(memory_space=pltpu.SMEM)
    vector = pl.BlockSpec(memory_space=pltpu.VMEM)
    half = jax.ShapeDtypeStruct((levels // 2, rows * cols), jnp.bfloat16)
    half_spec = pl.BlockSpec((levels // 2, chunk), lambda i: (0, i))
    return pl.pallas_call(
        functools.partial(localize_kernel, begin_row),
        grid=(rows // ROWS_PER_BLOCK,),
        out_shape=(half, half),
        in_specs=[scalars, scalars, vector, vector, vector,
                  pl.BlockSpec((1, levels, chunk), lambda i: (0, 0, i + skip))],
        out_specs=(half_spec, half_spec),
        scratch_shapes=[pltpu.VMEM((levels, chunk + 2 * cols), jnp.float32)],
        name="localize",
    )(place, tile_widths, arrived, weight, order, perturbations)


def body(
    alpha_weights, perturbations, coef_x, coef_y, level_scale, level_map, tile_widths, band_widths
):
    _, lev_dev, _, cols = alpha_weights.shape
    _, levels, capacity = perturbations.shape
    blocks = cols // LANES
    tiles = tile_widths.shape[0]
    mem = lax.axis_index("mem")
    place = lax.axis_index("lev").astype(jnp.int32).reshape(1)

    outgoing = smooth_and_cut(
        place, level_scale, level_map, tile_widths, alpha_weights, coef_x, coef_y, capacity
    )
    arrived = []
    for one in outgoing:
        if arrived:
            one, arrived[-1] = lax.optimization_barrier((one, arrived[-1]))
        one = lax.all_to_all(one, "lev", split_axis=0, concat_axis=0, tiled=True)
        arrived.append(one.reshape(tiles * SUBS, -1))

    slot = jnp.arange(levels)
    core = (mem + slot // 16) % CORES
    ring = (mem // CORES + (1 - 2 * core) * (slot // 4)) % RING
    half = (mem // (CORES * RING) + slot // 2) % HALVES
    row_level = half * 16 + ring * 4 + core * 2 + slot % 2
    order = (row_level[:, None] == slot[None, :]).astype(jnp.bfloat16)
    row_band = jnp.sum(jnp.where(row_level[:, None] == slot[None, :], band_widths[None, :], 0), 1)
    col_band = jnp.sum(jnp.where(level_map[:, None] == slot[None, :], band_widths[None, :], 0), 1)
    distance = jnp.abs(row_level[:, None] - level_map[None, :]).astype(jnp.float32)
    mutual = jnp.minimum(row_band[:, None], col_band[None, :]).astype(jnp.float32)
    local = jnp.where(distance <= mutual, jnp.exp(-distance * distance / (mutual * mutual)), 0.0)
    same_block = (jnp.arange(blocks)[:, None] == jnp.arange(blocks)[None, :])[:, None, None, :, None]
    weight = jnp.where(same_block, local.reshape(1, levels, tiles, 1, lev_dev), 0.0)
    weight = weight.astype(jnp.bfloat16).reshape(blocks * levels, tiles * SUBS)

    results = []
    begin = 0
    for rows_here, one in zip(PIECES, arrived):
        own, other = localize(
            begin, rows_here, place, tile_widths, one, weight, order, perturbations
        )
        results.append(sum_members(own, other))
        begin += rows_here
    return jnp.concatenate(results, axis=1)


def sum_members(own, other):
    def wide(x):
        return x.astype(jnp.float32)

    def narrow(x):
        return x.astype(jnp.bfloat16)

    def moved(dz, dx, dc):
        pairs = []
        for z in range(HALVES):
            for x in range(RING):
                for c in range(CORES):
                    along = dx * (1 - 2 * c)
                    to = ((z + dz) % HALVES, (x + along) % RING, (c + dc) % CORES)
                    pairs.append(((z * RING + x) * CORES + c, (to[0] * RING + to[1]) * CORES + to[2]))
        return pairs

    came = lax.ppermute(other, "mem", moved(0, 0, 1))
    pair = (wide(own) + wide(came)).reshape(RING, own.shape[0] // RING, own.shape[1])
    relay = lax.ppermute(narrow(pair[2]), "mem", moved(0, 1, 0))
    direct = lax.ppermute(narrow(pair[3]), "mem", moved(0, -1, 0))
    joined = lax.ppermute(narrow(pair[1] + wide(relay)), "mem", moved(0, 1, 0))
    total = pair[0] + wide(direct) + wide(joined)
    keep = total.shape[0] // HALVES
    far = lax.ppermute(narrow(total[keep:]), "mem", moved(1, 0, 0))
    return total[:keep] + wide(far)


def solution(mesh):
    placed = (P("mem", "lev", None, None), P("mem", None, "lev"), P(), P(), P(), P(), P(), P())

    return jax.shard_map(
        body, mesh=mesh, in_specs=placed, out_specs=P("mem", "lev"), check_vma=False
    )
```

```python
import functools

import jax
import jax.numpy as jnp
from jax import lax
from jax.experimental import pallas as pl
from jax.experimental.pallas import tpu as pltpu
from jax.sharding import PartitionSpec as P

STEPS = 16
LANES = 128
SUBS = 8
ROWS_PER_BLOCK = 8
PIECES = (24, 24)
CORES, RING, HALVES = 2, 4, 2


def split_bf16(x):
    high = x.astype(jnp.bfloat16)
    return high, (x - high.astype(jnp.float32)).astype(jnp.bfloat16)


def diffuse_kernel(
    place_ref, scale_ref, map_ref, width_ref, alpha_ref, cx_ref, cy_ref,
    out_ref, raw_scr, cx_scr, cy_scr, spread_ref, gather_ref, x_scr, f_scr, gx_scr, gy_scr, ax_scr,
    ay_scr, ayr_scr, o_scr, msg_scr, sems, out_sem,
):
    rows, cols = cx_ref.shape
    levels = alpha_ref.shape[1]
    fold = rows // SUBS
    blocks = cols // LANES
    tiles = width_ref.shape[0]

    def part(b):
        return pl.ds(b * LANES, LANES)

    copies = []
    for b in range(blocks):
        one = [
            pltpu.make_async_copy(cx_ref.at[:, part(b)], cx_scr.at[b], sems.at[b, 0]),
            pltpu.make_async_copy(cy_ref.at[:, part(b)], cy_scr.at[b], sems.at[b, 1]),
        ]
        for v in range(levels):
            one.append(
                pltpu.make_async_copy(
                    alpha_ref.at[0, v, :, part(b)], raw_scr.at[v, b], sems.at[b, 2 + v]
                )
            )
        copies.append(one)
    for k in range(2 + levels):
        for b in range(blocks):
            copies[b][k].start()

    for b in range(blocks):
        natural = lax.broadcasted_iota(jnp.int32, (cols, LANES), 0)
        spaced = lax.broadcasted_iota(jnp.int32, (cols, LANES), 1)
        match = jnp.where(natural == spaced * blocks + b, 1.0, 0.0)
        spread_ref[:, part(b)] = match.astype(jnp.bfloat16)
        match = jnp.where(natural % LANES * blocks + natural // LANES == spaced + b * LANES, 1.0, 0.0)
        gather_ref[:, part(b)] = match.astype(jnp.bfloat16)

    def spread_columns(planes):
        for r in range(fold):
            for b in range(blocks):
                x_scr[pl.ds(r * SUBS, SUBS), part(b)] = planes[b, pl.ds(r, SUBS, stride=fold), :]
        high, low = split_bf16(x_scr[...])
        return jnp.dot(high, spread_ref[...], preferred_element_type=jnp.float32) + jnp.dot(
            low, spread_ref[...], preferred_element_type=jnp.float32
        )

    lane = lax.broadcasted_iota(jnp.int32, (SUBS, LANES), 1)
    sub = lax.broadcasted_iota(jnp.int32, (SUBS, LANES), 0)
    for b in range(blocks):
        copies[b][0].wait()
    gx_scr[...] = spread_columns(cx_scr)
    for b in range(blocks):
        copies[b][1].wait()
    gy_scr[...] = spread_columns(cy_scr)

    def at(r):
        return pl.ds(r * SUBS, SUBS)

    for v in range(levels):
        gain = scale_ref[map_ref[place_ref[0] * levels + v]]
        for b in range(blocks):
            copies[b][2 + v].wait()
        f_scr[pl.ds(0, rows), :] = spread_columns(raw_scr.at[v])
        for r in range(fold):
            for b in range(blocks):
                ax = gx_scr[at(r), part(b)] * gain
                ay = gy_scr[at(r), part(b)] * gain
                if r == fold - 1:
                    ax = jnp.where(sub == SUBS - 1, 0.0, ax)
                if b == blocks - 1:
                    ay = jnp.where(lane == LANES - 1, 0.0, ay)
                    ayr_scr[at(r), :] = pltpu.roll(ay, 1, 1)
                ax_scr[at(r), part(b)] = ax
                ay_scr[at(r), part(b)] = ay

        @pl.loop(0, STEPS)
        def _(step):
            wrap = [pltpu.roll(f_scr[at(0), part(b)], SUBS - 1, 0) for b in range(blocks)]
            for b in range(blocks):
                f_scr[at(fold), part(b)] = wrap[b]
            here = [f_scr[at(fold - 1), part(b)] for b in range(blocks)]
            before = [
                pltpu.roll(ax_scr[at(fold - 1), part(b)] * (wrap[b] - here[b]), 1, 0)
                for b in range(blocks)
            ]
            here = [f_scr[at(0), part(b)] for b in range(blocks)]
            for r in range(fold):
                after = [f_scr[at(r + 1), part(b)] for b in range(blocks)]
                right = pltpu.roll(here[0], LANES - 1, 1)
                left = pltpu.roll(here[blocks - 1], 1, 1)
                last_y = ayr_scr[at(r), :] * (here[0] - left)
                flux = []
                for b in range(blocks):
                    fx = ax_scr[at(r), part(b)] * (after[b] - here[b])
                    beside = here[b + 1] if b < blocks - 1 else right
                    fy = ay_scr[at(r), part(b)] * (beside - here[b])
                    f_scr[at(r), part(b)] = here[b] + (fx - before[b]) + (fy - last_y)
                    last_y = fy
                    flux.append(fx)
                here, before = after, flux

        x_scr[...] = jnp.dot(
            f_scr[pl.ds(0, rows), :].astype(jnp.bfloat16),
            gather_ref[...],
            preferred_element_type=jnp.float32,
        )
        for r in range(fold):
            for b in range(blocks):
                o_scr[pl.ds(r * SUBS + b * levels + v, SUBS, stride=rows), :] = x_scr[at(r), part(b)]

    for i in range(rows):
        msg_scr[:, part(i)] = o_scr[at(i), :].astype(jnp.bfloat16)
    spare = msg_scr.shape[1] - rows * LANES
    msg_scr[:, pl.ds(rows * LANES, spare)] = jnp.zeros((SUBS, spare), jnp.bfloat16)
    sends = []
    first_col = 0
    for t in range(tiles):
        first = pl.multiple_of(first_col // cols * LANES, LANES)
        sends.append(
            pltpu.make_async_copy(
                msg_scr.at[:, pl.ds(first, out_ref.shape[2])], out_ref.at[t], out_sem.at[t]
            )
        )
        sends[-1].start()
        first_col = first_col + width_ref[t]
    for one in sends:
        one.wait()


def smooth_and_cut(place, level_scale, level_map, tile_widths, alpha, coef_x, coef_y, capacity):
    _, levels, rows, cols = alpha.shape
    tiles = tile_widths.shape[0]
    blocks = cols // LANES
    assert levels * blocks == SUBS and rows % SUBS == 0
    tile_rows = capacity // cols + 1
    assert sum(PIECES) == tile_rows - 1
    anywhere = pl.BlockSpec(memory_space=pl.ANY)
    scalars = pl.BlockSpec(memory_space=pltpu.SMEM)
    plane = pltpu.VMEM((blocks, rows, LANES), jnp.float32)
    whole = pltpu.VMEM((rows, cols), jnp.float32)
    square = pltpu.VMEM((cols, cols), jnp.bfloat16)
    return pl.pallas_call(
        diffuse_kernel,
        out_shape=jax.ShapeDtypeStruct((tiles, SUBS, tile_rows * LANES), jnp.bfloat16),
        in_specs=[scalars] * 4 + [anywhere] * 3,
        out_specs=anywhere,
        scratch_shapes=[
            pltpu.VMEM((levels, blocks, rows, LANES), jnp.float32),
            plane,
            plane,
            square,
            square,
            whole,
            pltpu.VMEM((rows + SUBS, cols), jnp.float32),
            whole,
            whole,
            whole,
            whole,
            pltpu.VMEM((rows, LANES), jnp.float32),
            pltpu.VMEM((rows * SUBS, LANES), jnp.float32),
            pltpu.VMEM((SUBS, (rows + tile_rows) * LANES), jnp.bfloat16),
            pltpu.SemaphoreType.DMA((blocks, 2 + levels)),
            pltpu.SemaphoreType.DMA((tiles,)),
        ],
        name="diffuse",
    )(place, level_scale, level_map, tile_widths, alpha, coef_x, coef_y)


def localize_kernel(
    begin_row, place_ref, width_ref, x_ref, weight_ref, order_ref, pert_ref, own_ref, send_ref, s_scr,
    here_scr, sem,
):
    step = pl.program_id(0)
    tiles = width_ref.shape[0]
    levels = order_ref.shape[0]
    blocks = weight_ref.shape[0] // levels
    cols = blocks * LANES
    chunk = pert_ref.shape[2]
    count = chunk // cols
    me = place_ref[0]
    first_col = 0
    for t in range(tiles):
        first_col = first_col + jnp.where(t < me, width_ref[t], 0)
    shift = first_col % cols
    shift_blocks = shift // LANES
    shift_lanes = shift % LANES
    width = width_ref[me] - begin_row * cols - step * chunk
    begin = pl.multiple_of(step * (count * LANES), LANES)

    @pl.when(step == 0)
    def _():
        rows_here = pl.ds(begin_row * LANES, here_scr.shape[1])
        copy = pltpu.make_async_copy(x_ref.at[:, rows_here], here_scr, sem)
        copy.start()
        copy.wait()

    spread = jnp.dot(
        weight_ref[...],
        here_scr[:, pl.ds(begin, (count + 1) * LANES)],
        preferred_element_type=jnp.float32,
    )
    for r in range(count + 1):
        for b in range(blocks):
            s_scr[:, pl.ds((r * blocks + b) * LANES, LANES)] = spread[
                b * levels : (b + 1) * levels, r * LANES : (r + 1) * LANES
            ]
    ordered = jnp.dot(order_ref[...], pert_ref[0], preferred_element_type=jnp.float32)
    lane = lax.broadcasted_iota(jnp.int32, (levels, LANES), 1)
    keep = lane < LANES - shift_lanes
    half = levels // 2

    def rolled(k):
        block = s_scr[:, pl.ds(pl.multiple_of((k + shift_blocks) * LANES, LANES), LANES)]
        return pltpu.roll(block, lax.rem(LANES - shift_lanes, LANES), 1)

    here = rolled(0)
    for k in range(count * blocks):
        after = rolled(k + 1)
        at = jnp.where(keep, here, after)
        part = pl.ds(k * LANES, LANES)
        value = ordered[:, k * LANES : (k + 1) * LANES] * at
        value = jnp.where(lane < width - k * LANES, value, 0.0).astype(jnp.bfloat16)
        own_ref[:, part] = value[:half]
        send_ref[:, part] = value[half:]
        here = after


def localize(begin_row, rows, place, tile_widths, arrived, weight, order, perturbations):
    levels = perturbations.shape[1]
    blocks = weight.shape[0] // levels
    cols = blocks * LANES
    chunk = ROWS_PER_BLOCK * cols
    assert rows % ROWS_PER_BLOCK == 0 and begin_row % ROWS_PER_BLOCK == 0
    skip = begin_row // ROWS_PER_BLOCK
    scalars = pl.BlockSpec(memory_space=pltpu.SMEM)
    vector = pl.BlockSpec(memory_space=pltpu.VMEM)
    half = jax.ShapeDtypeStruct((levels // 2, rows * cols), jnp.bfloat16)
    half_spec = pl.BlockSpec((levels // 2, chunk), lambda i: (0, i))
    return pl.pallas_call(
        functools.partial(localize_kernel, begin_row),
        grid=(rows // ROWS_PER_BLOCK,),
        out_shape=(half, half),
        in_specs=[scalars, scalars, pl.BlockSpec(memory_space=pl.ANY), vector, vector,
                  pl.BlockSpec((1, levels, chunk), lambda i: (0, 0, i + skip))],
        out_specs=(half_spec, half_spec),
        scratch_shapes=[
            pltpu.VMEM((levels, chunk + 2 * cols), jnp.float32),
            pltpu.VMEM((arrived.shape[0], (rows + 1) * LANES), jnp.bfloat16),
            pltpu.SemaphoreType.DMA,
        ],
        compiler_params=pltpu.CompilerParams(vmem_limit_bytes=16 << 20),
        name="localize",
    )(place, tile_widths, arrived, weight, order, perturbations)


def body(
    alpha_weights, perturbations, coef_x, coef_y, level_scale, level_map, tile_widths, band_widths
):
    _, lev_dev, _, cols = alpha_weights.shape
    _, levels, capacity = perturbations.shape
    blocks = cols // LANES
    tiles = tile_widths.shape[0]
    mem = lax.axis_index("mem")
    place = lax.axis_index("lev").astype(jnp.int32).reshape(1)

    outgoing = smooth_and_cut(
        place, level_scale, level_map, tile_widths, alpha_weights, coef_x, coef_y, capacity
    )
    arrived = lax.all_to_all(outgoing, "lev", split_axis=0, concat_axis=0, tiled=True)
    arrived = arrived.reshape(tiles * SUBS, -1)

    slot = jnp.arange(levels)
    core = (mem + slot // 16) % CORES
    ring = (mem // CORES + slot // 4) % RING
    half = (mem // (CORES * RING) + slot // 2) % HALVES
    row_level = half * 16 + ring * 4 + core * 2 + slot % 2
    order = (row_level[:, None] == slot[None, :]).astype(jnp.bfloat16)
    row_band = jnp.sum(jnp.where(row_level[:, None] == slot[None, :], band_widths[None, :], 0), 1)
    col_band = jnp.sum(jnp.where(level_map[:, None] == slot[None, :], band_widths[None, :], 0), 1)
    distance = jnp.abs(row_level[:, None] - level_map[None, :]).astype(jnp.float32)
    mutual = jnp.minimum(row_band[:, None], col_band[None, :]).astype(jnp.float32)
    local = jnp.where(distance <= mutual, jnp.exp(-distance * distance / (mutual * mutual)), 0.0)
    same_block = (jnp.arange(blocks)[:, None] == jnp.arange(blocks)[None, :])[:, None, None, :, None]
    weight = jnp.where(same_block, local.reshape(1, levels, tiles, 1, lev_dev), 0.0)
    weight = weight.astype(jnp.bfloat16).reshape(blocks * levels, tiles * SUBS)

    results = []
    begin = 0
    for rows_here in PIECES:
        own, other = localize(
            begin, rows_here, place, tile_widths, arrived, weight, order, perturbations
        )
        results.append(sum_members(own, other))
        begin += rows_here
    return jnp.concatenate(results, axis=1)


def sum_members(own, other):
    def wide(x):
        return x.astype(jnp.float32)

    def narrow(x):
        return x.astype(jnp.bfloat16)

    def moved(dz, dx, dc):
        pairs = []
        for z in range(HALVES):
            for x in range(RING):
                for c in range(CORES):
                    to = ((z + dz) % HALVES, (x + dx) % RING, (c + dc) % CORES)
                    pairs.append(((z * RING + x) * CORES + c, (to[0] * RING + to[1]) * CORES + to[2]))
        return pairs

    keep = own.shape[0] // RING
    came = lax.ppermute(other, "mem", moved(0, 0, 1))
    total = wide(own[:keep]) + wide(came[:keep])
    pair = narrow(wide(own[keep:]) + wide(came[keep:])).reshape(RING - 1, keep, -1)
    around = [lax.ppermute(pair[d - 1], "mem", moved(0, d, 0)) for d in range(1, RING)]
    for one in around:
        total = total + wide(one)
    keep //= HALVES
    far = lax.ppermute(narrow(total[keep:]), "mem", moved(1, 0, 0))
    return total[:keep] + wide(far)


def solution(mesh):
    placed = (P("mem", "lev", None, None), P("mem", None, "lev"), P(), P(), P(), P(), P(), P())

    return jax.shard_map(
        body, mesh=mesh, in_specs=placed, out_specs=P("mem", "lev"), check_vma=False
    )
```

```python
import functools

import jax
import jax.numpy as jnp
from jax import lax
from jax.experimental import pallas as pl
from jax.experimental.pallas import tpu as pltpu
from jax.sharding import PartitionSpec as P

STEPS = 16
LANES = 128
SUBS = 8
ROWS_PER_BLOCK = 8
PIECES = (24, 24)
CORES, RING, HALVES = 2, 4, 2


def split_bf16(x):
    high = x.astype(jnp.bfloat16)
    return high, (x - high.astype(jnp.float32)).astype(jnp.bfloat16)


def diffuse_kernel(
    place_ref, scale_ref, map_ref, width_ref, alpha_ref, cx_ref, cy_ref,
    out_ref, raw_scr, cx_scr, cy_scr, spread_ref, gather_ref, x_scr, f_scr, gx_scr, gy_scr, ax_scr,
    ay_scr, ayr_scr, o_scr, msg_scr, sems, out_sem,
):
    rows, cols = cx_ref.shape
    levels = alpha_ref.shape[1]
    fold = rows // SUBS
    blocks = cols // LANES
    tiles = width_ref.shape[0]

    def part(b):
        return pl.ds(b * LANES, LANES)

    copies = []
    for b in range(blocks):
        one = [
            pltpu.make_async_copy(cx_ref.at[:, part(b)], cx_scr.at[b], sems.at[b, 0]),
            pltpu.make_async_copy(cy_ref.at[:, part(b)], cy_scr.at[b], sems.at[b, 1]),
        ]
        for v in range(levels):
            one.append(
                pltpu.make_async_copy(
                    alpha_ref.at[0, v, :, part(b)], raw_scr.at[v, b], sems.at[b, 2 + v]
                )
            )
        copies.append(one)
    for k in range(2 + levels):
        for b in range(blocks):
            copies[b][k].start()

    for b in range(blocks):
        natural = lax.broadcasted_iota(jnp.int32, (cols, LANES), 0)
        spaced = lax.broadcasted_iota(jnp.int32, (cols, LANES), 1)
        match = jnp.where(natural == spaced * blocks + b, 1.0, 0.0)
        spread_ref[:, part(b)] = match.astype(jnp.bfloat16)
        match = jnp.where(natural % LANES * blocks + natural // LANES == spaced + b * LANES, 1.0, 0.0)
        gather_ref[:, part(b)] = match.astype(jnp.bfloat16)

    def spread_columns(planes):
        for r in range(fold):
            for b in range(blocks):
                x_scr[pl.ds(r * SUBS, SUBS), part(b)] = planes[b, pl.ds(r, SUBS, stride=fold), :]
        high, low = split_bf16(x_scr[...])
        return jnp.dot(high, spread_ref[...], preferred_element_type=jnp.float32) + jnp.dot(
            low, spread_ref[...], preferred_element_type=jnp.float32
        )

    lane = lax.broadcasted_iota(jnp.int32, (SUBS, LANES), 1)
    sub = lax.broadcasted_iota(jnp.int32, (SUBS, LANES), 0)
    for b in range(blocks):
        copies[b][0].wait()
    gx_scr[...] = spread_columns(cx_scr)
    for b in range(blocks):
        copies[b][1].wait()
    gy_scr[...] = spread_columns(cy_scr)

    def at(r):
        return pl.ds(r * SUBS, SUBS)

    for v in range(levels):
        gain = scale_ref[map_ref[place_ref[0] * levels + v]]
        for b in range(blocks):
            copies[b][2 + v].wait()
        f_scr[pl.ds(0, rows), :] = spread_columns(raw_scr.at[v])
        for r in range(fold):
            for b in range(blocks):
                ax = gx_scr[at(r), part(b)] * gain
                ay = gy_scr[at(r), part(b)] * gain
                if r == fold - 1:
                    ax = jnp.where(sub == SUBS - 1, 0.0, ax)
                if b == blocks - 1:
                    ay = jnp.where(lane == LANES - 1, 0.0, ay)
                    ayr_scr[at(r), :] = pltpu.roll(ay, 1, 1)
                ax_scr[at(r), part(b)] = ax
                ay_scr[at(r), part(b)] = ay

        @pl.loop(0, STEPS)
        def _(step):
            wrap = [pltpu.roll(f_scr[at(0), part(b)], SUBS - 1, 0) for b in range(blocks)]
            for b in range(blocks):
                f_scr[at(fold), part(b)] = wrap[b]
            here = [f_scr[at(fold - 1), part(b)] for b in range(blocks)]
            before = [
                pltpu.roll(ax_scr[at(fold - 1), part(b)] * (wrap[b] - here[b]), 1, 0)
                for b in range(blocks)
            ]
            here = [f_scr[at(0), part(b)] for b in range(blocks)]
            for r in range(fold):
                after = [f_scr[at(r + 1), part(b)] for b in range(blocks)]
                right = pltpu.roll(here[0], LANES - 1, 1)
                left = pltpu.roll(here[blocks - 1], 1, 1)
                last_y = ayr_scr[at(r), :] * (here[0] - left)
                flux = []
                for b in range(blocks):
                    fx = ax_scr[at(r), part(b)] * (after[b] - here[b])
                    beside = here[b + 1] if b < blocks - 1 else right
                    fy = ay_scr[at(r), part(b)] * (beside - here[b])
                    f_scr[at(r), part(b)] = here[b] + (fx - before[b]) + (fy - last_y)
                    last_y = fy
                    flux.append(fx)
                here, before = after, flux

        natural = jnp.dot(
            f_scr[pl.ds(0, rows), :].astype(jnp.bfloat16),
            gather_ref[...],
            preferred_element_type=jnp.float32,
        )
        for r in range(fold):
            for b in range(blocks):
                o_scr[at(r * SUBS + b * levels + v), :] = natural[
                    r * SUBS : (r + 1) * SUBS, b * LANES : (b + 1) * LANES
                ]

    for r in range(fold):
        for i in range(SUBS):
            row = o_scr[pl.ds(r * SUBS * SUBS + i, SUBS, stride=SUBS), :]
            msg_scr[:, part(i * fold + r)] = row.astype(jnp.bfloat16)
    spare = msg_scr.shape[1] - rows * LANES
    msg_scr[:, pl.ds(rows * LANES, spare)] = jnp.zeros((SUBS, spare), jnp.bfloat16)
    sends = []
    first_col = 0
    for t in range(tiles):
        first = pl.multiple_of(first_col // cols * LANES, LANES)
        sends.append(
            pltpu.make_async_copy(
                msg_scr.at[:, pl.ds(first, out_ref.shape[2])], out_ref.at[t], out_sem.at[t]
            )
        )
        sends[-1].start()
        first_col = first_col + width_ref[t]
    for one in sends:
        one.wait()


def smooth_and_cut(place, level_scale, level_map, tile_widths, alpha, coef_x, coef_y, capacity):
    _, levels, rows, cols = alpha.shape
    tiles = tile_widths.shape[0]
    blocks = cols // LANES
    assert levels * blocks == SUBS and rows % SUBS == 0
    tile_rows = capacity // cols + 1
    assert sum(PIECES) == tile_rows - 1
    anywhere = pl.BlockSpec(memory_space=pl.ANY)
    scalars = pl.BlockSpec(memory_space=pltpu.SMEM)
    plane = pltpu.VMEM((blocks, rows, LANES), jnp.float32)
    whole = pltpu.VMEM((rows, cols), jnp.float32)
    square = pltpu.VMEM((cols, cols), jnp.bfloat16)
    return pl.pallas_call(
        diffuse_kernel,
        out_shape=jax.ShapeDtypeStruct((tiles, SUBS, tile_rows * LANES), jnp.bfloat16),
        in_specs=[scalars] * 4 + [anywhere] * 3,
        out_specs=anywhere,
        scratch_shapes=[
            pltpu.VMEM((levels, blocks, rows, LANES), jnp.float32),
            plane,
            plane,
            square,
            square,
            whole,
            pltpu.VMEM((rows + SUBS, cols), jnp.float32),
            whole,
            whole,
            whole,
            whole,
            pltpu.VMEM((rows, LANES), jnp.float32),
            pltpu.VMEM((rows * SUBS, LANES), jnp.float32),
            pltpu.VMEM((SUBS, (rows + tile_rows) * LANES), jnp.bfloat16),
            pltpu.SemaphoreType.DMA((blocks, 2 + levels)),
            pltpu.SemaphoreType.DMA((tiles,)),
        ],
        name="diffuse",
    )(place, level_scale, level_map, tile_widths, alpha, coef_x, coef_y)


def localize_kernel(
    begin_row, place_ref, width_ref, x_ref, weight_ref, order_ref, pert_ref, own_ref, send_ref, s_scr,
    here_scr, sem,
):
    step = pl.program_id(0)
    tiles = width_ref.shape[0]
    levels = order_ref.shape[0]
    blocks = weight_ref.shape[0] // levels
    cols = blocks * LANES
    chunk = pert_ref.shape[2]
    count = chunk // cols
    me = place_ref[0]
    first_col = 0
    for t in range(tiles):
        first_col = first_col + jnp.where(t < me, width_ref[t], 0)
    shift = first_col % cols
    shift_blocks = shift // LANES
    shift_lanes = shift % LANES
    width = width_ref[me] - begin_row * cols - step * chunk
    begin = pl.multiple_of(step * (count * LANES), LANES)

    @pl.when(step == 0)
    def _():
        rows_here = pl.ds(begin_row * LANES, here_scr.shape[1])
        copy = pltpu.make_async_copy(x_ref.at[:, rows_here], here_scr, sem)
        copy.start()
        copy.wait()

    spread = jnp.dot(
        weight_ref[...],
        here_scr[:, pl.ds(begin, (count + 1) * LANES)],
        preferred_element_type=jnp.float32,
    )
    for r in range(count + 1):
        for b in range(blocks):
            s_scr[:, pl.ds((r * blocks + b) * LANES, LANES)] = spread[
                b * levels : (b + 1) * levels, r * LANES : (r + 1) * LANES
            ]
    ordered = jnp.dot(order_ref[...], pert_ref[0], preferred_element_type=jnp.float32)
    lane = lax.broadcasted_iota(jnp.int32, (levels, LANES), 1)
    keep = lane < LANES - shift_lanes
    half = levels // 2

    def rolled(k):
        block = s_scr[:, pl.ds(pl.multiple_of((k + shift_blocks) * LANES, LANES), LANES)]
        return pltpu.roll(block, lax.rem(LANES - shift_lanes, LANES), 1)

    here = rolled(0)
    for k in range(count * blocks):
        after = rolled(k + 1)
        at = jnp.where(keep, here, after)
        part = pl.ds(k * LANES, LANES)
        value = ordered[:, k * LANES : (k + 1) * LANES] * at
        value = jnp.where(lane < width - k * LANES, value, 0.0).astype(jnp.bfloat16)
        own_ref[:, part] = value[:half]
        send_ref[:, part] = value[half:]
        here = after


def localize(begin_row, rows, place, tile_widths, arrived, weight, order, perturbations):
    levels = perturbations.shape[1]
    blocks = weight.shape[0] // levels
    cols = blocks * LANES
    chunk = ROWS_PER_BLOCK * cols
    assert rows % ROWS_PER_BLOCK == 0 and begin_row % ROWS_PER_BLOCK == 0
    skip = begin_row // ROWS_PER_BLOCK
    scalars = pl.BlockSpec(memory_space=pltpu.SMEM)
    vector = pl.BlockSpec(memory_space=pltpu.VMEM)
    half = jax.ShapeDtypeStruct((levels // 2, rows * cols), jnp.bfloat16)
    half_spec = pl.BlockSpec((levels // 2, chunk), lambda i: (0, i))
    return pl.pallas_call(
        functools.partial(localize_kernel, begin_row),
        grid=(rows // ROWS_PER_BLOCK,),
        out_shape=(half, half),
        in_specs=[scalars, scalars, pl.BlockSpec(memory_space=pl.ANY), vector, vector,
                  pl.BlockSpec((1, levels, chunk), lambda i: (0, 0, i + skip))],
        out_specs=(half_spec, half_spec),
        scratch_shapes=[
            pltpu.VMEM((levels, chunk + 2 * cols), jnp.float32),
            pltpu.VMEM((arrived.shape[0], (rows + 1) * LANES), jnp.bfloat16),
            pltpu.SemaphoreType.DMA,
        ],
        compiler_params=pltpu.CompilerParams(vmem_limit_bytes=16 << 20),
        name="localize",
    )(place, tile_widths, arrived, weight, order, perturbations)


def body(
    alpha_weights, perturbations, coef_x, coef_y, level_scale, level_map, tile_widths, band_widths
):
    _, lev_dev, _, cols = alpha_weights.shape
    _, levels, capacity = perturbations.shape
    blocks = cols // LANES
    tiles = tile_widths.shape[0]
    mem = lax.axis_index("mem")
    place = lax.axis_index("lev").astype(jnp.int32).reshape(1)

    outgoing = smooth_and_cut(
        place, level_scale, level_map, tile_widths, alpha_weights, coef_x, coef_y, capacity
    )
    arrived = lax.all_to_all(outgoing, "lev", split_axis=0, concat_axis=0, tiled=True)
    arrived = arrived.reshape(tiles * SUBS, -1)

    slot = jnp.arange(levels)
    core = (mem + slot // 16) % CORES
    ring = (mem // CORES + (1 - 2 * core) * (slot // 4)) % RING
    half = (mem // (CORES * RING) + slot // 2) % HALVES
    row_level = half * 16 + ring * 4 + core * 2 + slot % 2
    order = (row_level[:, None] == slot[None, :]).astype(jnp.bfloat16)
    row_band = jnp.sum(jnp.where(row_level[:, None] == slot[None, :], band_widths[None, :], 0), 1)
    col_band = jnp.sum(jnp.where(level_map[:, None] == slot[None, :], band_widths[None, :], 0), 1)
    distance = jnp.abs(row_level[:, None] - level_map[None, :]).astype(jnp.float32)
    mutual = jnp.minimum(row_band[:, None], col_band[None, :]).astype(jnp.float32)
    local = jnp.where(distance <= mutual, jnp.exp(-distance * distance / (mutual * mutual)), 0.0)
    same_block = (jnp.arange(blocks)[:, None] == jnp.arange(blocks)[None, :])[:, None, None, :, None]
    weight = jnp.where(same_block, local.reshape(1, levels, tiles, 1, lev_dev), 0.0)
    weight = weight.astype(jnp.bfloat16).reshape(blocks * levels, tiles * SUBS)

    results = []
    begin = 0
    for rows_here in PIECES:
        own, other = localize(
            begin, rows_here, place, tile_widths, arrived, weight, order, perturbations
        )
        results.append(sum_members(own, other))
        begin += rows_here
    return jnp.concatenate(results, axis=1)


def sum_members(own, other):
    def wide(x):
        return x.astype(jnp.float32)

    def narrow(x):
        return x.astype(jnp.bfloat16)

    def moved(dz, dx, dc):
        pairs = []
        for z in range(HALVES):
            for x in range(RING):
                for c in range(CORES):
                    along = dx * (1 - 2 * c)
                    to = ((z + dz) % HALVES, (x + along) % RING, (c + dc) % CORES)
                    pairs.append(((z * RING + x) * CORES + c, (to[0] * RING + to[1]) * CORES + to[2]))
        return pairs

    keep = own.shape[0] // RING
    came = lax.ppermute(other, "mem", moved(0, 0, 1))
    total = wide(own[:keep]) + wide(came[:keep])
    beside = wide(own[keep : 2 * keep]) + wide(came[keep : 2 * keep])
    pair = narrow(wide(own[2 * keep :]) + wide(came[2 * keep :]))
    relay = lax.ppermute(pair[:keep], "mem", moved(0, 1, 0))
    direct = lax.ppermute(pair[keep:], "mem", moved(0, -1, 0))
    joined = lax.ppermute(narrow(beside + wide(relay)), "mem", moved(0, 1, 0))
    total = total + wide(direct) + wide(joined)
    keep //= HALVES
    far = lax.ppermute(narrow(total[keep:]), "mem", moved(1, 0, 0))
    return total[:keep] + wide(far)


def solution(mesh):
    placed = (P("mem", "lev", None, None), P("mem", None, "lev"), P(), P(), P(), P(), P(), P())

    return jax.shard_map(
        body, mesh=mesh, in_specs=placed, out_specs=P("mem", "lev"), check_vma=False
    )
```

```python
import functools

import jax
import jax.numpy as jnp
from jax import lax
from jax.experimental import pallas as pl
from jax.experimental.pallas import tpu as pltpu
from jax.sharding import PartitionSpec as P

STEPS = 16
LANES = 128
SUBS = 8
ROWS_PER_BLOCK = 8
PIECES = (24, 24)
LINE = 4
ROUND = 64
ROUNDS = 2
CORES, RING, HALVES = 2, 4, 2


def split_bf16(x):
    high = x.astype(jnp.bfloat16)
    return high, (x - high.astype(jnp.float32)).astype(jnp.bfloat16)


def diffuse_kernel(
    place_ref, scale_ref, map_ref, width_ref, alpha_ref, cx_ref, cy_ref,
    out_ref, *refs,
):
    late_refs, more_ref = refs[: LINE * ROUNDS], refs[LINE * ROUNDS]
    (
        raw_scr, cx_scr, cy_scr, spread_ref, gather_ref, x_scr, f_scr, gx_scr, gy_scr, ax_scr,
        ay_scr, ayr_scr, o_scr, msg_scr, late_scr, sems, out_sem, late_sem,
    ) = refs[LINE * ROUNDS + 1 :]
    rows, cols = cx_ref.shape
    levels = alpha_ref.shape[1]
    fold = rows // SUBS
    blocks = cols // LANES
    tiles = width_ref.shape[0]

    def part(b):
        return pl.ds(b * LANES, LANES)

    copies = []
    for b in range(blocks):
        one = [
            pltpu.make_async_copy(cx_ref.at[:, part(b)], cx_scr.at[b], sems.at[b, 0]),
            pltpu.make_async_copy(cy_ref.at[:, part(b)], cy_scr.at[b], sems.at[b, 1]),
        ]
        for v in range(levels):
            one.append(
                pltpu.make_async_copy(
                    alpha_ref.at[0, v, :, part(b)], raw_scr.at[v, b], sems.at[b, 2 + v]
                )
            )
        copies.append(one)
    for k in range(2 + levels):
        for b in range(blocks):
            copies[b][k].start()

    for b in range(blocks):
        natural = lax.broadcasted_iota(jnp.int32, (cols, LANES), 0)
        spaced = lax.broadcasted_iota(jnp.int32, (cols, LANES), 1)
        match = jnp.where(natural == spaced * blocks + b, 1.0, 0.0)
        spread_ref[:, part(b)] = match.astype(jnp.bfloat16)
        match = jnp.where(natural % LANES * blocks + natural // LANES == spaced + b * LANES, 1.0, 0.0)
        gather_ref[:, part(b)] = match.astype(jnp.bfloat16)

    def spread_columns(planes):
        for r in range(fold):
            for b in range(blocks):
                x_scr[pl.ds(r * SUBS, SUBS), part(b)] = planes[b, pl.ds(r, SUBS, stride=fold), :]
        high, low = split_bf16(x_scr[...])
        return jnp.dot(high, spread_ref[...], preferred_element_type=jnp.float32) + jnp.dot(
            low, spread_ref[...], preferred_element_type=jnp.float32
        )

    lane = lax.broadcasted_iota(jnp.int32, (SUBS, LANES), 1)
    sub = lax.broadcasted_iota(jnp.int32, (SUBS, LANES), 0)
    for b in range(blocks):
        copies[b][0].wait()
    gx_scr[...] = spread_columns(cx_scr)
    for b in range(blocks):
        copies[b][1].wait()
    gy_scr[...] = spread_columns(cy_scr)

    def at(r):
        return pl.ds(r * SUBS, SUBS)

    for v in range(levels):
        gain = scale_ref[map_ref[place_ref[0] * levels + v]]
        for b in range(blocks):
            copies[b][2 + v].wait()
        f_scr[pl.ds(0, rows), :] = spread_columns(raw_scr.at[v])
        for r in range(fold):
            for b in range(blocks):
                ax = gx_scr[at(r), part(b)] * gain
                ay = gy_scr[at(r), part(b)] * gain
                if r == fold - 1:
                    ax = jnp.where(sub == SUBS - 1, 0.0, ax)
                if b == blocks - 1:
                    ay = jnp.where(lane == LANES - 1, 0.0, ay)
                    ayr_scr[at(r), :] = pltpu.roll(ay, 1, 1)
                ax_scr[at(r), part(b)] = ax
                ay_scr[at(r), part(b)] = ay

        @pl.loop(0, STEPS)
        def _(step):
            wrap = [pltpu.roll(f_scr[at(0), part(b)], SUBS - 1, 0) for b in range(blocks)]
            for b in range(blocks):
                f_scr[at(fold), part(b)] = wrap[b]
            here = [f_scr[at(fold - 1), part(b)] for b in range(blocks)]
            before = [
                pltpu.roll(ax_scr[at(fold - 1), part(b)] * (wrap[b] - here[b]), 1, 0)
                for b in range(blocks)
            ]
            here = [f_scr[at(0), part(b)] for b in range(blocks)]
            for r in range(fold):
                after = [f_scr[at(r + 1), part(b)] for b in range(blocks)]
                right = pltpu.roll(here[0], LANES - 1, 1)
                left = pltpu.roll(here[blocks - 1], 1, 1)
                last_y = ayr_scr[at(r), :] * (here[0] - left)
                flux = []
                for b in range(blocks):
                    fx = ax_scr[at(r), part(b)] * (after[b] - here[b])
                    beside = here[b + 1] if b < blocks - 1 else right
                    fy = ay_scr[at(r), part(b)] * (beside - here[b])
                    f_scr[at(r), part(b)] = here[b] + (fx - before[b]) + (fy - last_y)
                    last_y = fy
                    flux.append(fx)
                here, before = after, flux

        natural = jnp.dot(
            f_scr[pl.ds(0, rows), :].astype(jnp.bfloat16),
            gather_ref[...],
            preferred_element_type=jnp.float32,
        )
        for r in range(fold):
            for b in range(blocks):
                o_scr[at(r * SUBS + b * levels + v), :] = natural[
                    r * SUBS : (r + 1) * SUBS, b * LANES : (b + 1) * LANES
                ]

    for r in range(fold):
        for i in range(SUBS):
            row = o_scr[pl.ds(r * SUBS * SUBS + i, SUBS, stride=SUBS), :]
            msg_scr[:, part(i * fold + r)] = row.astype(jnp.bfloat16)
    spare = msg_scr.shape[1] - rows * LANES
    msg_scr[:, pl.ds(rows * LANES, spare)] = jnp.zeros((SUBS, spare), jnp.bfloat16)
    sends = []
    first_col = 0
    for t in range(tiles):
        first = pl.multiple_of(first_col // cols * LANES, LANES)
        sends.append(
            pltpu.make_async_copy(
                msg_scr.at[:, pl.ds(first, out_ref.shape[2])], out_ref.at[t], out_sem.at[t]
            )
        )
        sends[-1].start()
        first_col = first_col + width_ref[t]
    more = 0
    tall = PIECES[0] + 1
    for d in range(LINE):
        plane = lax.rem(place_ref[0] + d, LINE)
        filled = 0
        for k in range(tiles // LINE):
            first_col, count = late_rows(width_ref, k * LINE + plane, cols)
            first = pl.multiple_of((first_col // cols + PIECES[0]) * LANES, LANES)
            to = pl.multiple_of(filled * LANES, LANES)
            late_scr[d, :, pl.ds(to, tall * LANES)] = msg_scr[:, pl.ds(first, tall * LANES)]
            filled = filled + count
        more = jnp.maximum(more, filled)
    more_ref[0] = more
    for k in range(ROUNDS):
        for d in range(LINE):
            span = pl.ds(k * ROUND * LANES, ROUND * LANES)
            sends.append(
                pltpu.make_async_copy(
                    late_scr.at[d, :, span], late_refs[k * LINE + d], late_sem.at[k, d]
                )
            )
            sends[-1].start()
    for one in sends:
        one.wait()


def late_rows(width_ref, tile, cols):
    first_col = 0
    for t in range(width_ref.shape[0]):
        first_col = first_col + jnp.where(t < tile, width_ref[t], 0)
    width = width_ref[tile]
    rows = (first_col + width - 1) // cols - first_col // cols + 1 - PIECES[0]
    return first_col, jnp.where(width > PIECES[0] * cols, rows, 0)


def smooth_and_cut(place, level_scale, level_map, tile_widths, alpha, coef_x, coef_y, capacity):
    _, levels, rows, cols = alpha.shape
    tiles = tile_widths.shape[0]
    blocks = cols // LANES
    assert levels * blocks == SUBS and rows % SUBS == 0
    tile_rows = capacity // cols + 1
    assert sum(PIECES) == tile_rows - 1 and PIECES[0] == PIECES[1]
    assert tiles // LINE * (PIECES[0] + 1) <= ROUNDS * ROUND
    anywhere = pl.BlockSpec(memory_space=pl.ANY)
    scalars = pl.BlockSpec(memory_space=pltpu.SMEM)
    plane = pltpu.VMEM((blocks, rows, LANES), jnp.float32)
    whole = pltpu.VMEM((rows, cols), jnp.float32)
    square = pltpu.VMEM((cols, cols), jnp.bfloat16)
    return pl.pallas_call(
        diffuse_kernel,
        out_shape=[
            jax.ShapeDtypeStruct((tiles, SUBS, (PIECES[0] + 1) * LANES), jnp.bfloat16),
            *[jax.ShapeDtypeStruct((SUBS, ROUND * LANES), jnp.bfloat16)] * (LINE * ROUNDS),
            jax.ShapeDtypeStruct((1,), jnp.int32),
        ],
        in_specs=[scalars] * 4 + [anywhere] * 3,
        out_specs=[anywhere] * (1 + LINE * ROUNDS) + [scalars],
        scratch_shapes=[
            pltpu.VMEM((levels, blocks, rows, LANES), jnp.float32),
            plane,
            plane,
            square,
            square,
            whole,
            pltpu.VMEM((rows + SUBS, cols), jnp.float32),
            whole,
            whole,
            whole,
            whole,
            pltpu.VMEM((rows, LANES), jnp.float32),
            pltpu.VMEM((rows * SUBS, LANES), jnp.float32),
            pltpu.VMEM((SUBS, (rows + tile_rows) * LANES), jnp.bfloat16),
            pltpu.VMEM((LINE, SUBS, ROUNDS * ROUND * LANES), jnp.bfloat16),
            pltpu.SemaphoreType.DMA((blocks, 2 + levels)),
            pltpu.SemaphoreType.DMA((tiles,)),
            pltpu.SemaphoreType.DMA((ROUNDS, LINE)),
        ],
        name="diffuse",
    )(place, level_scale, level_map, tile_widths, alpha, coef_x, coef_y)


def regroup_kernel(cols, place_ref, width_ref, *refs):
    come_refs = refs[: LINE * ROUNDS]
    out_refs = refs[LINE * ROUNDS : -3]
    held_scr, in_sem, out_sem = refs[-3:]
    tall = PIECES[0] + 1
    copies = []
    for k in range(ROUNDS):
        for d in range(LINE):
            span = pl.ds(k * ROUND * LANES, ROUND * LANES)
            copies.append(
                pltpu.make_async_copy(
                    come_refs[k * LINE + d], held_scr.at[d, :, span], in_sem.at[k, d]
                )
            )
            copies[-1].start()
    for copy in copies:
        copy.wait()
    plane = lax.rem(place_ref[0], LINE)
    groups = len(out_refs)
    starts = [0]
    for k in range(groups - 1):
        starts.append(starts[-1] + late_rows(width_ref, k * LINE + plane, cols)[1])
    copies = []
    for e in range(groups):
        group = lax.rem(place_ref[0] // LINE + e, groups)
        first = 0
        for k in range(groups):
            first = jnp.where(group == k, starts[k], first)
        first = pl.multiple_of(first * LANES, LANES)
        for d in range(LINE):
            copies.append(
                pltpu.make_async_copy(
                    held_scr.at[d, :, pl.ds(first, tall * LANES)], out_refs[e].at[d], out_sem.at[e, d]
                )
            )
            copies[-1].start()
    for copy in copies:
        copy.wait()


def regroup(place, tile_widths, come, cols):
    groups = tile_widths.shape[0] // LINE
    scalars = pl.BlockSpec(memory_space=pltpu.SMEM)
    anywhere = pl.BlockSpec(memory_space=pl.ANY)
    one = jax.ShapeDtypeStruct((LINE, SUBS, (PIECES[0] + 1) * LANES), jnp.bfloat16)
    return pl.pallas_call(
        functools.partial(regroup_kernel, cols),
        out_shape=[one] * groups,
        in_specs=[scalars] * 2 + [anywhere] * len(come),
        out_specs=[anywhere] * groups,
        scratch_shapes=[
            pltpu.VMEM((LINE, SUBS, ROUNDS * ROUND * LANES), jnp.bfloat16),
            pltpu.SemaphoreType.DMA((ROUNDS, LINE)),
            pltpu.SemaphoreType.DMA((groups, LINE)),
        ],
        compiler_params=pltpu.CompilerParams(vmem_limit_bytes=8 << 20),
        name="regroup",
    )(place, tile_widths, *come)


def localize_kernel(
    begin_row, sources, place_ref, width_ref, *refs
):
    x_refs = refs[:sources]
    weight_ref, order_ref, pert_ref, own_ref, send_ref, s_scr, here_scr, sem = refs[sources:]
    step = pl.program_id(0)
    tiles = width_ref.shape[0]
    levels = order_ref.shape[0]
    blocks = weight_ref.shape[0] // levels
    cols = blocks * LANES
    chunk = pert_ref.shape[2]
    count = chunk // cols
    me = place_ref[0]
    first_col = 0
    for t in range(tiles):
        first_col = first_col + jnp.where(t < me, width_ref[t], 0)
    shift = first_col % cols
    shift_blocks = shift // LANES
    shift_lanes = shift % LANES
    width = width_ref[me] - begin_row * cols - step * chunk
    begin = pl.multiple_of(step * (count * LANES), LANES)

    @pl.when(step == 0)
    def _():
        depth = here_scr.shape[0] // sources
        copies = [
            pltpu.make_async_copy(x_ref, here_scr.at[pl.ds(k * depth, depth), :], sem.at[k])
            for k, x_ref in enumerate(x_refs)
        ]
        for copy in copies:
            copy.start()
        for copy in copies:
            copy.wait()

    spread = jnp.dot(
        weight_ref[...],
        here_scr[:, pl.ds(begin, (count + 1) * LANES)],
        preferred_element_type=jnp.float32,
    )
    for r in range(count + 1):
        for b in range(blocks):
            s_scr[:, pl.ds((r * blocks + b) * LANES, LANES)] = spread[
                b * levels : (b + 1) * levels, r * LANES : (r + 1) * LANES
            ]
    ordered = jnp.dot(order_ref[...], pert_ref[0], preferred_element_type=jnp.float32)
    lane = lax.broadcasted_iota(jnp.int32, (levels, LANES), 1)
    keep = lane < LANES - shift_lanes
    half = levels // 2

    def rolled(k):
        block = s_scr[:, pl.ds(pl.multiple_of((k + shift_blocks) * LANES, LANES), LANES)]
        return pltpu.roll(block, lax.rem(LANES - shift_lanes, LANES), 1)

    here = rolled(0)
    for k in range(count * blocks):
        after = rolled(k + 1)
        at = jnp.where(keep, here, after)
        part = pl.ds(k * LANES, LANES)
        value = ordered[:, k * LANES : (k + 1) * LANES] * at
        value = jnp.where(lane < width - k * LANES, value, 0.0).astype(jnp.bfloat16)
        own_ref[:, part] = value[:half]
        send_ref[:, part] = value[half:]
        here = after


def localize(begin_row, rows, place, tile_widths, arrived, weight, order, perturbations):
    levels = perturbations.shape[1]
    blocks = weight.shape[0] // levels
    cols = blocks * LANES
    chunk = ROWS_PER_BLOCK * cols
    assert rows % ROWS_PER_BLOCK == 0 and begin_row % ROWS_PER_BLOCK == 0
    skip = begin_row // ROWS_PER_BLOCK
    scalars = pl.BlockSpec(memory_space=pltpu.SMEM)
    vector = pl.BlockSpec(memory_space=pltpu.VMEM)
    half = jax.ShapeDtypeStruct((levels // 2, rows * cols), jnp.bfloat16)
    half_spec = pl.BlockSpec((levels // 2, chunk), lambda i: (0, i))
    return pl.pallas_call(
        functools.partial(localize_kernel, begin_row, len(arrived)),
        grid=(rows // ROWS_PER_BLOCK,),
        out_shape=(half, half),
        in_specs=[scalars] * 2 + [pl.BlockSpec(memory_space=pl.ANY)] * len(arrived) + [vector, vector,
                  pl.BlockSpec((1, levels, chunk), lambda i: (0, 0, i + skip))],
        out_specs=(half_spec, half_spec),
        scratch_shapes=[
            pltpu.VMEM((levels, chunk + 2 * cols), jnp.float32),
            pltpu.VMEM((weight.shape[1], (rows + 1) * LANES), jnp.bfloat16),
            pltpu.SemaphoreType.DMA((len(arrived),)),
        ],
        compiler_params=pltpu.CompilerParams(vmem_limit_bytes=16 << 20),
        name="localize",
    )(place, tile_widths, *arrived, weight, order, perturbations)


def body(
    alpha_weights, perturbations, coef_x, coef_y, level_scale, level_map, tile_widths, band_widths
):
    _, lev_dev, _, cols = alpha_weights.shape
    _, levels, capacity = perturbations.shape
    blocks = cols // LANES
    tiles = tile_widths.shape[0]
    mem = lax.axis_index("mem")
    place = lax.axis_index("lev").astype(jnp.int32).reshape(1)

    groups = tiles // LINE
    outgoing, *late, more = smooth_and_cut(
        place, level_scale, level_map, tile_widths, alpha_weights, coef_x, coef_y, capacity
    )

    def shifted(dy, dz):
        return [
            (y * LINE + z, (y + dy) % groups * LINE + (z + dz) % LINE)
            for y in range(groups)
            for z in range(LINE)
        ]

    def along_line(planes):
        came = [planes[0]]
        for d in range(1, LINE):
            came.append(lax.ppermute(planes[d], "lev", shifted(0, d)))
        return tuple(came)

    come = along_line(late[:LINE])
    arrived = lax.all_to_all(outgoing, "lev", split_axis=0, concat_axis=0, tiled=True)
    arrived = arrived.reshape(tiles * SUBS, -1)
    for k in range(1, ROUNDS):
        rest = tuple(late[k * LINE : (k + 1) * LINE])
        come += lax.cond(more[0] > k * ROUND, along_line, lambda planes: planes, rest)
    grouped = regroup(place, tile_widths, come, cols)
    joined = [grouped[0]]
    for d in range(1, groups):
        joined.append(lax.ppermute(grouped[d], "lev", shifted(d, 0)))
    joined = [one.reshape(LINE * SUBS, -1) for one in joined]
    inputs = ([arrived], joined)

    slot = jnp.arange(levels)
    core = (mem + slot // 16) % CORES
    ring = (mem // CORES + (1 - 2 * core) * (slot // 4)) % RING
    half = (mem // (CORES * RING) + slot // 2) % HALVES
    row_level = half * 16 + ring * 4 + core * 2 + slot % 2
    order = (row_level[:, None] == slot[None, :]).astype(jnp.bfloat16)
    row_band = jnp.sum(jnp.where(row_level[:, None] == slot[None, :], band_widths[None, :], 0), 1)
    at = jnp.arange(tiles)
    near = (place[0] // LINE - at // LINE) % groups * LINE + (place[0] - at) % LINE
    near = (near[:, None] * lev_dev + jnp.arange(lev_dev)[None, :]).reshape(-1)
    near_map = jnp.sum(jnp.where(near[:, None] == slot[None, :], level_map[None, :], 0), 1)

    def weight_of(col_level):
        col_band = jnp.sum(
            jnp.where(col_level[:, None] == slot[None, :], band_widths[None, :], 0), 1
        )
        distance = jnp.abs(row_level[:, None] - col_level[None, :]).astype(jnp.float32)
        mutual = jnp.minimum(row_band[:, None], col_band[None, :]).astype(jnp.float32)
        local = jnp.where(distance <= mutual, jnp.exp(-distance * distance / (mutual * mutual)), 0.0)
        same = (jnp.arange(blocks)[:, None] == jnp.arange(blocks)[None, :])[:, None, None, :, None]
        weight = jnp.where(same, local.reshape(1, levels, tiles, 1, lev_dev), 0.0)
        return weight.astype(jnp.bfloat16).reshape(blocks * levels, tiles * SUBS)

    weights = (weight_of(level_map), weight_of(near_map))

    results = []
    begin = 0
    for p, rows_here in enumerate(PIECES):
        own, other = localize(
            begin, rows_here, place, tile_widths, inputs[p], weights[p], order, perturbations
        )
        results.append(sum_members(own, other))
        begin += rows_here
    return jnp.concatenate(results, axis=1)


def sum_members(own, other):
    def wide(x):
        return x.astype(jnp.float32)

    def narrow(x):
        return x.astype(jnp.bfloat16)

    def moved(dz, dx, dc):
        pairs = []
        for z in range(HALVES):
            for x in range(RING):
                for c in range(CORES):
                    along = dx * (1 - 2 * c)
                    to = ((z + dz) % HALVES, (x + along) % RING, (c + dc) % CORES)
                    pairs.append(((z * RING + x) * CORES + c, (to[0] * RING + to[1]) * CORES + to[2]))
        return pairs

    keep = own.shape[0] // RING
    came = lax.ppermute(other, "mem", moved(0, 0, 1))
    total = wide(own[:keep]) + wide(came[:keep])
    beside = wide(own[keep : 2 * keep]) + wide(came[keep : 2 * keep])
    pair = narrow(wide(own[2 * keep :]) + wide(came[2 * keep :]))
    relay = lax.ppermute(pair[:keep], "mem", moved(0, 1, 0))
    direct = lax.ppermute(pair[keep:], "mem", moved(0, -1, 0))
    joined = lax.ppermute(narrow(beside + wide(relay)), "mem", moved(0, 1, 0))
    total = total + wide(direct) + wide(joined)
    keep //= HALVES
    far = lax.ppermute(narrow(total[keep:]), "mem", moved(1, 0, 0))
    return total[:keep] + wide(far)


def solution(mesh):
    placed = (P("mem", "lev", None, None), P("mem", None, "lev"), P(), P(), P(), P(), P(), P())

    return jax.shard_map(
        body, mesh=mesh, in_specs=placed, out_specs=P("mem", "lev"), check_vma=False
    )
```

```python
import functools

import jax
import jax.numpy as jnp
from jax import lax
from jax.experimental import pallas as pl
from jax.experimental.pallas import tpu as pltpu
from jax.sharding import PartitionSpec as P

STEPS = 16
LANES = 128
SUBS = 8
ROWS_PER_BLOCK = 8
CORES, RING, HALVES = 2, 4, 2
PIECES = (24, 24)
LINE = 4


def split_bf16(x):
    high = x.astype(jnp.bfloat16)
    return high, (x - high.astype(jnp.float32)).astype(jnp.bfloat16)


def diffuse_kernel(
    level, place_ref, scale_ref, map_ref, width_ref, alpha_ref, cx_ref, cy_ref, *refs
):
    out_refs = refs[:-15]
    (
        raw_scr, cx_scr, cy_scr, spread_scr, gather_scr, x_scr, f_scr, ax_scr, ay_scr, ayr_scr,
        o_scr, msg_scr, starts, sems, out_sem,
    ) = refs[-15:]
    rows, cols = cx_ref.shape
    levels = alpha_ref.shape[1]
    fold = rows // SUBS
    blocks = cols // LANES
    pack = SUBS // blocks
    tiles = width_ref.shape[0]

    def part(b):
        return pl.ds(b * LANES, LANES)

    def at(r):
        return pl.ds(r * SUBS, SUBS)

    sources = (cx_ref, cy_ref, alpha_ref.at[0, level])
    planes = (cx_scr, cy_scr, raw_scr)
    copies = [
        [
            pltpu.make_async_copy(source.at[:, part(b)], plane.at[b], sems.at[k, b])
            for b in range(blocks)
        ]
        for k, (source, plane) in enumerate(zip(sources, planes))
    ]
    for one in copies:
        for copy in one:
            copy.start()

    for b in range(blocks):
        natural = lax.broadcasted_iota(jnp.int32, (cols, LANES), 0)
        spaced = lax.broadcasted_iota(jnp.int32, (cols, LANES), 1)
        match = jnp.where(natural == spaced * blocks + b, 1.0, 0.0)
        spread_scr[:, part(b)] = match.astype(jnp.bfloat16)
        match = jnp.where(natural % LANES * blocks + natural // LANES == spaced + b * LANES, 1.0, 0.0)
        gather_scr[:, part(b)] = match.astype(jnp.bfloat16)

    def spread_columns(k):
        for copy in copies[k]:
            copy.wait()
        for r in range(fold):
            for b in range(blocks):
                x_scr[at(r), part(b)] = planes[k][b, pl.ds(r, SUBS, stride=fold), :]
        high, low = split_bf16(x_scr[...])
        return jnp.dot(high, spread_scr[...], preferred_element_type=jnp.float32) + jnp.dot(
            low, spread_scr[...], preferred_element_type=jnp.float32
        )

    lane = lax.broadcasted_iota(jnp.int32, (SUBS, LANES), 1)
    sub = lax.broadcasted_iota(jnp.int32, (SUBS, LANES), 0)
    gain = scale_ref[map_ref[place_ref[0] * levels + level]]
    ax_scr[...] = spread_columns(0) * gain
    ay_scr[...] = spread_columns(1) * gain
    for b in range(blocks):
        ax_scr[at(fold - 1), part(b)] = jnp.where(
            sub == SUBS - 1, 0.0, ax_scr[at(fold - 1), part(b)]
        )
    for r in range(fold):
        ay = jnp.where(lane == LANES - 1, 0.0, ay_scr[at(r), part(blocks - 1)])
        ay_scr[at(r), part(blocks - 1)] = ay
        ayr_scr[at(r), :] = pltpu.roll(ay, 1, 1)
    f_scr[pl.ds(0, rows), :] = spread_columns(2)

    @pl.loop(0, STEPS)
    def _(step):
        wrap = [pltpu.roll(f_scr[at(0), part(b)], SUBS - 1, 0) for b in range(blocks)]
        for b in range(blocks):
            f_scr[at(fold), part(b)] = wrap[b]
        here = [f_scr[at(fold - 1), part(b)] for b in range(blocks)]
        before = [
            pltpu.roll(ax_scr[at(fold - 1), part(b)] * (wrap[b] - here[b]), 1, 0)
            for b in range(blocks)
        ]
        here = [f_scr[at(0), part(b)] for b in range(blocks)]
        for r in range(fold):
            after = [f_scr[at(r + 1), part(b)] for b in range(blocks)]
            right = pltpu.roll(here[0], LANES - 1, 1)
            left = pltpu.roll(here[blocks - 1], 1, 1)
            last_y = ayr_scr[at(r), :] * (here[0] - left)
            flux = []
            for b in range(blocks):
                fx = ax_scr[at(r), part(b)] * (after[b] - here[b])
                beside = here[b + 1] if b < blocks - 1 else right
                fy = ay_scr[at(r), part(b)] * (beside - here[b])
                f_scr[at(r), part(b)] = here[b] + (fx - before[b]) + (fy - last_y)
                last_y = fy
                flux.append(fx)
            here, before = after, flux

    natural = jnp.dot(
        f_scr[pl.ds(0, rows), :].astype(jnp.bfloat16),
        gather_scr[...],
        preferred_element_type=jnp.float32,
    )
    for r in range(fold):
        for b in range(blocks):
            o_scr[at(r * blocks + b), :] = natural[
                r * SUBS : (r + 1) * SUBS, b * LANES : (b + 1) * LANES
            ]
    for r in range(fold // pack):
        for i in range(SUBS):
            row = o_scr[pl.ds(r * SUBS * SUBS + i, SUBS, stride=SUBS), :]
            msg_scr[:, part(i * (fold // pack) + r)] = row.astype(jnp.bfloat16)
    used = rows // pack * LANES
    msg_scr[:, pl.ds(used, msg_scr.shape[1] - used)] = jnp.zeros(
        (SUBS, msg_scr.shape[1] - used), jnp.bfloat16
    )
    first_col = 0
    for t in range(tiles):
        starts[t] = first_col
        first_col = first_col + width_ref[t]
    sends = []
    groups = tiles // LINE
    for k in range(tiles):
        d, e = k // groups, k % groups
        if len(out_refs) > 1:
            tile = lax.rem(place_ref[0] // LINE + e, groups) * LINE + lax.rem(place_ref[0] + d, LINE)
            target = out_refs[d].at[e]
        else:
            tile, target = k, out_refs[0].at[k]
        first = pl.multiple_of(starts[tile] // (cols * pack) * LANES, LANES)
        sends.append(
            pltpu.make_async_copy(
                msg_scr.at[:, pl.ds(first, out_refs[0].shape[2])], target, out_sem.at[k]
            )
        )
        sends[-1].start()
    for one in sends:
        one.wait()


def smooth_and_cut(level, place, level_scale, level_map, tile_widths, alpha, coef_x, coef_y, tall):
    rows, cols = alpha.shape[2:]
    tiles = tile_widths.shape[0]
    blocks = cols // LANES
    pack = SUBS // blocks
    assert SUBS % blocks == 0 and rows % (SUBS * pack) == 0
    anywhere = pl.BlockSpec(memory_space=pl.ANY)
    scalars = pl.BlockSpec(memory_space=pltpu.SMEM)
    plane = pltpu.VMEM((blocks, rows, LANES), jnp.float32)
    whole = pltpu.VMEM((rows, cols), jnp.float32)
    square = pltpu.VMEM((cols, cols), jnp.bfloat16)
    split = LINE if level == 0 else 1
    return pl.pallas_call(
        functools.partial(diffuse_kernel, level),
        out_shape=[
            jax.ShapeDtypeStruct((tiles // split, SUBS, (tall // pack + 1) * LANES), jnp.bfloat16)
        ]
        * split,
        in_specs=[scalars] * 4 + [anywhere] * 3,
        out_specs=[anywhere] * split,
        scratch_shapes=[
            plane,
            plane,
            plane,
            square,
            square,
            whole,
            pltpu.VMEM((rows + SUBS, cols), jnp.float32),
            whole,
            whole,
            pltpu.VMEM((rows, LANES), jnp.float32),
            pltpu.VMEM((rows * blocks, LANES), jnp.float32),
            pltpu.VMEM((SUBS, ((rows + tall) // pack + 1) * LANES), jnp.bfloat16),
            pltpu.SMEM((tiles,), jnp.int32),
            pltpu.SemaphoreType.DMA((3, blocks)),
            pltpu.SemaphoreType.DMA((tiles,)),
        ],
        name="diffuse",
    )(place, level_scale, level_map, tile_widths, alpha, coef_x, coef_y)


def localize_kernel(
    begin_row, cols, parts, place_ref, width_ref, *refs
):
    x_refs = refs[: sum(parts)]
    weight_ref, order_ref, pert_ref, own_ref, send_ref, s_scr, here_scr, sem = refs[sum(parts) :]
    step = pl.program_id(0)
    tiles = width_ref.shape[0]
    levels = order_ref.shape[0]
    blocks = cols // LANES
    group = weight_ref.shape[1] // levels
    pack = group // blocks
    chunk = pert_ref.shape[2]
    count = chunk // (cols * pack)
    me = place_ref[0]
    first_col = 0
    for t in range(tiles):
        first_col = first_col + jnp.where(t < me, width_ref[t], 0)
    shift = first_col % (cols * pack)
    shift_blocks = shift // LANES
    shift_lanes = shift % LANES
    width = width_ref[me] - begin_row * cols - step * chunk

    @pl.when(step == 0)
    def _():
        lanes = pl.ds(begin_row // pack * LANES, here_scr.shape[2])
        copies = []
        for v, n in enumerate(parts):
            depth = here_scr.shape[1] // n
            for k in range(n):
                m = len(copies)
                target = here_scr.at[v, pl.ds(k * depth, depth), :]
                copies.append(pltpu.make_async_copy(x_refs[m].at[:, lanes], target, sem.at[m]))
                copies[-1].start()
        for copy in copies:
            copy.wait()

    spread = 0.0
    first = pl.multiple_of(step * (count * LANES), LANES)
    for v in range(len(parts)):
        spread = spread + jnp.dot(
            weight_ref[v],
            here_scr[v, :, pl.ds(first, (count + 1) * LANES)],
            preferred_element_type=jnp.float32,
        )
    for r in range(count + 1):
        for b in range(group):
            s_scr[:, pl.ds((r * group + b) * LANES, LANES)] = spread[
                b * levels : (b + 1) * levels, r * LANES : (r + 1) * LANES
            ]
    ordered = jnp.dot(order_ref[...], pert_ref[0], preferred_element_type=jnp.float32)
    lane = lax.broadcasted_iota(jnp.int32, (levels, LANES), 1)
    keep = lane < LANES - shift_lanes
    half = levels // 2

    def rolled(k):
        block = s_scr[:, pl.ds(pl.multiple_of((k + shift_blocks) * LANES, LANES), LANES)]
        return pltpu.roll(block, lax.rem(LANES - shift_lanes, LANES), 1)

    here = rolled(0)
    for k in range(count * group):
        after = rolled(k + 1)
        at = jnp.where(keep, here, after)
        part = pl.ds(k * LANES, LANES)
        value = ordered[:, k * LANES : (k + 1) * LANES] * at
        value = jnp.where(lane < width - k * LANES, value, 0.0).astype(jnp.bfloat16)
        own_ref[:, part] = value[:half]
        send_ref[:, part] = value[half:]
        here = after


def localize(begin_row, rows, cols, place, tile_widths, arrived, weight, order, perturbations):
    levels = perturbations.shape[1]
    chunk = ROWS_PER_BLOCK * cols
    assert rows % ROWS_PER_BLOCK == 0 and begin_row % ROWS_PER_BLOCK == 0
    skip = begin_row // ROWS_PER_BLOCK
    group = weight.shape[1] // levels
    parts = tuple(len(one) for one in arrived)
    scalars = pl.BlockSpec(memory_space=pltpu.SMEM)
    vector = pl.BlockSpec(memory_space=pltpu.VMEM)
    half = jax.ShapeDtypeStruct((levels // 2, rows * cols), jnp.bfloat16)
    half_spec = pl.BlockSpec((levels // 2, chunk), lambda i: (0, i))
    return pl.pallas_call(
        functools.partial(localize_kernel, begin_row, cols, parts),
        grid=(rows // ROWS_PER_BLOCK,),
        out_shape=(half, half),
        in_specs=[scalars] * 2 + [pl.BlockSpec(memory_space=pl.ANY)] * sum(parts) + [vector, vector,
                  pl.BlockSpec((1, levels, chunk), lambda i: (0, 0, i + skip))],
        out_specs=(half_spec, half_spec),
        scratch_shapes=[
            pltpu.VMEM((levels, chunk + group * LANES), jnp.float32),
            pltpu.VMEM(
                (len(parts), weight.shape[2], (rows // (group * LANES // cols) + 1) * LANES),
                jnp.bfloat16,
            ),
            pltpu.SemaphoreType.DMA((sum(parts),)),
        ],
        compiler_params=pltpu.CompilerParams(vmem_limit_bytes=16 << 20),
        name="localize",
    )(place, tile_widths, *sum(map(list, arrived), []), weight, order, perturbations)


def body(
    alpha_weights, perturbations, coef_x, coef_y, level_scale, level_map, tile_widths, band_widths
):
    _, lev_dev, _, cols = alpha_weights.shape
    _, levels, capacity = perturbations.shape
    tiles = tile_widths.shape[0]
    tall = capacity // cols
    assert sum(PIECES) == tall and lev_dev == 2
    groups = tiles // LINE
    mem = lax.axis_index("mem")
    place = lax.axis_index("lev").astype(jnp.int32).reshape(1)

    def shifted(dy, dz):
        return [
            (y * LINE + z, (y + dy) % groups * LINE + (z + dz) % LINE)
            for y in range(groups)
            for z in range(LINE)
        ]

    def smooth(v):
        return smooth_and_cut(
            v, place, level_scale, level_map, tile_widths, alpha_weights, coef_x, coef_y, tall
        )

    planes = smooth(0)
    come = [planes[0]]
    for d in range(1, LINE):
        come.append(lax.ppermute(planes[d], "lev", shifted(0, d)))
    outgoing = smooth(1)[0]
    arrived = lax.all_to_all(outgoing, "lev", split_axis=0, concat_axis=0, tiled=True)
    joined = []
    for e in range(groups):
        one = jnp.concatenate([plane[e] for plane in come], axis=0)
        if e > 0:
            one = lax.ppermute(one, "lev", shifted(e, 0))
        joined.append(one)
    inputs = (joined, [arrived.reshape(tiles * SUBS, -1)])

    slot = jnp.arange(levels)
    core = (mem + slot // 16) % CORES
    ring = (mem // CORES + (1 - 2 * core) * (slot // 4)) % RING
    half = (mem // (CORES * RING) + slot // 2) % HALVES
    row_level = half * 16 + ring * 4 + core * 2 + slot % 2
    order = (row_level[:, None] == slot[None, :]).astype(jnp.bfloat16)
    row_band = jnp.sum(jnp.where(row_level[:, None] == slot[None, :], band_widths[None, :], 0), 1)
    at = jnp.arange(tiles)
    near = (place[0] // LINE - at // LINE) % groups * LINE + (place[0] - at) % LINE
    col_slot = jnp.stack([near * lev_dev, at * lev_dev + 1])
    match = col_slot[:, :, None] == slot
    col_level = jnp.sum(jnp.where(match, level_map, 0), 2)
    match = col_level[:, :, None] == slot
    col_band = jnp.sum(jnp.where(match, band_widths, 0), 2)
    distance = jnp.abs(row_level[None, :, None] - col_level[:, None, :]).astype(jnp.float32)
    mutual = jnp.minimum(row_band[None, :, None], col_band[:, None, :]).astype(jnp.float32)
    local = jnp.where(distance <= mutual, jnp.exp(-distance * distance / (mutual * mutual)), 0.0)
    group = jnp.arange(SUBS)
    same = (group[:, None, None, None] == group).reshape(1, SUBS, 1, 1, SUBS)
    weight = jnp.where(same, local[:, None, :, :, None], 0.0).astype(jnp.bfloat16)
    weight = weight.reshape(lev_dev, SUBS * levels, tiles * SUBS)

    results = []
    begin = 0
    for rows_here in PIECES:
        own, other = localize(
            begin, rows_here, cols, place, tile_widths, inputs, weight, order, perturbations
        )
        results.append(sum_members(own, other))
        begin += rows_here
    return jnp.concatenate(results, axis=1)


def sum_members(own, other):
    def wide(x):
        return x.astype(jnp.float32)

    def narrow(x):
        return x.astype(jnp.bfloat16)

    def moved(dz, dx, dc):
        pairs = []
        for z in range(HALVES):
            for x in range(RING):
                for c in range(CORES):
                    along = dx * (1 - 2 * c)
                    to = ((z + dz) % HALVES, (x + along) % RING, (c + dc) % CORES)
                    pairs.append(((z * RING + x) * CORES + c, (to[0] * RING + to[1]) * CORES + to[2]))
        return pairs

    keep = own.shape[0] // RING
    came = lax.ppermute(other, "mem", moved(0, 0, 1))
    total = wide(own[:keep]) + wide(came[:keep])
    beside = wide(own[keep : 2 * keep]) + wide(came[keep : 2 * keep])
    pair = narrow(wide(own[2 * keep :]) + wide(came[2 * keep :]))
    relay = lax.ppermute(pair[:keep], "mem", moved(0, 1, 0))
    direct = lax.ppermute(pair[keep:], "mem", moved(0, -1, 0))
    joined = lax.ppermute(narrow(beside + wide(relay)), "mem", moved(0, 1, 0))
    total = total + wide(direct) + wide(joined)
    keep //= HALVES
    far = lax.ppermute(narrow(total[keep:]), "mem", moved(1, 0, 0))
    return total[:keep] + wide(far)


def solution(mesh):
    placed = (P("mem", "lev", None, None), P("mem", None, "lev"), P(), P(), P(), P(), P(), P())

    return jax.shard_map(
        body, mesh=mesh, in_specs=placed, out_specs=P("mem", "lev"), check_vma=False
    )
```

```python
import functools

import jax
import jax.numpy as jnp
from jax import lax
from jax.experimental import pallas as pl
from jax.experimental.pallas import tpu as pltpu
from jax.sharding import PartitionSpec as P

STEPS = 16
LANES = 128
SUBS = 8
ROWS_PER_BLOCK = 8
CORES, RING, HALVES = 2, 4, 2
PIECES = (24, 24)
LINE = 4


def split_bf16(x):
    high = x.astype(jnp.bfloat16)
    return high, (x - high.astype(jnp.float32)).astype(jnp.bfloat16)


def diffuse_kernel(
    level, place_ref, scale_ref, map_ref, width_ref, alpha_ref, cx_ref, cy_ref, *refs
):
    out_refs = refs[:-15]
    (
        raw_scr, cx_scr, cy_scr, spread_scr, gather_scr, x_scr, f_scr, ax_scr, ay_scr, ayr_scr,
        o_scr, msg_scr, starts, sems, out_sem,
    ) = refs[-15:]
    rows, cols = cx_ref.shape
    levels = alpha_ref.shape[1]
    fold = rows // SUBS
    blocks = cols // LANES
    pack = SUBS // blocks
    tiles = width_ref.shape[0]

    def part(b):
        return pl.ds(b * LANES, LANES)

    def at(r):
        return pl.ds(r * SUBS, SUBS)

    sources = (cx_ref, cy_ref, alpha_ref.at[0, level])
    planes = (cx_scr, cy_scr, raw_scr)
    copies = [
        [
            pltpu.make_async_copy(source.at[:, part(b)], plane.at[b], sems.at[k, b])
            for b in range(blocks)
        ]
        for k, (source, plane) in enumerate(zip(sources, planes))
    ]
    for one in copies:
        for copy in one:
            copy.start()

    for b in range(blocks):
        natural = lax.broadcasted_iota(jnp.int32, (cols, LANES), 0)
        spaced = lax.broadcasted_iota(jnp.int32, (cols, LANES), 1)
        match = jnp.where(natural == spaced * blocks + b, 1.0, 0.0)
        spread_scr[:, part(b)] = match.astype(jnp.bfloat16)
        match = jnp.where(natural % LANES * blocks + natural // LANES == spaced + b * LANES, 1.0, 0.0)
        gather_scr[:, part(b)] = match.astype(jnp.bfloat16)

    def spread_columns(k):
        for copy in copies[k]:
            copy.wait()
        for r in range(fold):
            for b in range(blocks):
                x_scr[at(r), part(b)] = planes[k][b, pl.ds(r, SUBS, stride=fold), :]
        high, low = split_bf16(x_scr[...])
        return jnp.dot(high, spread_scr[...], preferred_element_type=jnp.float32) + jnp.dot(
            low, spread_scr[...], preferred_element_type=jnp.float32
        )

    lane = lax.broadcasted_iota(jnp.int32, (SUBS, LANES), 1)
    sub = lax.broadcasted_iota(jnp.int32, (SUBS, LANES), 0)
    gain = scale_ref[map_ref[place_ref[0] * levels + level]]
    ax_scr[...] = spread_columns(0) * gain
    ay_scr[...] = spread_columns(1) * gain
    for b in range(blocks):
        ax_scr[at(fold - 1), part(b)] = jnp.where(
            sub == SUBS - 1, 0.0, ax_scr[at(fold - 1), part(b)]
        )
    for r in range(fold):
        ay = jnp.where(lane == LANES - 1, 0.0, ay_scr[at(r), part(blocks - 1)])
        ay_scr[at(r), part(blocks - 1)] = ay
        ayr_scr[at(r), :] = pltpu.roll(ay, 1, 1)
    f_scr[pl.ds(0, rows), :] = spread_columns(2)

    @pl.loop(0, STEPS)
    def _(step):
        wrap = [pltpu.roll(f_scr[at(0), part(b)], SUBS - 1, 0) for b in range(blocks)]
        for b in range(blocks):
            f_scr[at(fold), part(b)] = wrap[b]
        here = [f_scr[at(fold - 1), part(b)] for b in range(blocks)]
        before = [
            pltpu.roll(ax_scr[at(fold - 1), part(b)] * (wrap[b] - here[b]), 1, 0)
            for b in range(blocks)
        ]
        here = [f_scr[at(0), part(b)] for b in range(blocks)]
        for r in range(fold):
            after = [f_scr[at(r + 1), part(b)] for b in range(blocks)]
            right = pltpu.roll(here[0], LANES - 1, 1)
            left = pltpu.roll(here[blocks - 1], 1, 1)
            last_y = ayr_scr[at(r), :] * (here[0] - left)
            flux = []
            for b in range(blocks):
                fx = ax_scr[at(r), part(b)] * (after[b] - here[b])
                beside = here[b + 1] if b < blocks - 1 else right
                fy = ay_scr[at(r), part(b)] * (beside - here[b])
                f_scr[at(r), part(b)] = here[b] + (fx - before[b]) + (fy - last_y)
                last_y = fy
                flux.append(fx)
            here, before = after, flux

    natural = jnp.dot(
        f_scr[pl.ds(0, rows), :].astype(jnp.bfloat16),
        gather_scr[...],
        preferred_element_type=jnp.float32,
    )
    for r in range(fold):
        for b in range(blocks):
            o_scr[at(r * blocks + b), :] = natural[
                r * SUBS : (r + 1) * SUBS, b * LANES : (b + 1) * LANES
            ]
    for r in range(fold // pack):
        for i in range(SUBS):
            row = o_scr[pl.ds(r * SUBS * SUBS + i, SUBS, stride=SUBS), :]
            msg_scr[:, part(i * (fold // pack) + r)] = row.astype(jnp.bfloat16)
    used = rows // pack * LANES
    msg_scr[:, pl.ds(used, msg_scr.shape[1] - used)] = jnp.zeros(
        (SUBS, msg_scr.shape[1] - used), jnp.bfloat16
    )
    first_col = 0
    for t in range(tiles):
        starts[t] = first_col
        first_col = first_col + width_ref[t]
    sends = []
    groups = tiles // LINE
    for k in range(tiles):
        d, e = k // groups, k % groups
        if len(out_refs) > 1:
            tile = lax.rem(place_ref[0] // LINE + e, groups) * LINE + lax.rem(place_ref[0] + d, LINE)
            target = out_refs[d].at[e]
        else:
            tile, target = k, out_refs[0].at[k]
        first = pl.multiple_of(starts[tile] // (cols * pack) * LANES, LANES)
        sends.append(
            pltpu.make_async_copy(
                msg_scr.at[:, pl.ds(first, out_refs[0].shape[2])], target, out_sem.at[k]
            )
        )
        sends[-1].start()
    for one in sends:
        one.wait()


def smooth_and_cut(level, place, level_scale, level_map, tile_widths, alpha, coef_x, coef_y, tall):
    rows, cols = alpha.shape[2:]
    tiles = tile_widths.shape[0]
    blocks = cols // LANES
    pack = SUBS // blocks
    assert SUBS % blocks == 0 and rows % (SUBS * pack) == 0
    anywhere = pl.BlockSpec(memory_space=pl.ANY)
    scalars = pl.BlockSpec(memory_space=pltpu.SMEM)
    plane = pltpu.VMEM((blocks, rows, LANES), jnp.float32)
    whole = pltpu.VMEM((rows, cols), jnp.float32)
    square = pltpu.VMEM((cols, cols), jnp.bfloat16)
    split = LINE if level == 0 else 1
    return pl.pallas_call(
        functools.partial(diffuse_kernel, level),
        out_shape=[
            jax.ShapeDtypeStruct((tiles // split, SUBS, (tall // pack + 1) * LANES), jnp.bfloat16)
        ]
        * split,
        in_specs=[scalars] * 4 + [anywhere] * 3,
        out_specs=[anywhere] * split,
        scratch_shapes=[
            plane,
            plane,
            plane,
            square,
            square,
            whole,
            pltpu.VMEM((rows + SUBS, cols), jnp.float32),
            whole,
            whole,
            pltpu.VMEM((rows, LANES), jnp.float32),
            pltpu.VMEM((rows * blocks, LANES), jnp.float32),
            pltpu.VMEM((SUBS, ((rows + tall) // pack + 1) * LANES), jnp.bfloat16),
            pltpu.SMEM((tiles,), jnp.int32),
            pltpu.SemaphoreType.DMA((3, blocks)),
            pltpu.SemaphoreType.DMA((tiles,)),
        ],
        name="diffuse",
    )(place, level_scale, level_map, tile_widths, alpha, coef_x, coef_y)


def localize_kernel(
    begin_row, cols, parts, place_ref, width_ref, *refs
):
    x_refs = refs[: sum(parts)]
    weight_ref, order_ref, pert_ref, own_ref, send_ref, s_scr, here_scr, sem = refs[sum(parts) :]
    step = pl.program_id(0)
    tiles = width_ref.shape[0]
    levels = order_ref.shape[0]
    blocks = cols // LANES
    group = weight_ref.shape[1] // levels
    pack = group // blocks
    chunk = pert_ref.shape[2]
    count = chunk // (cols * pack)
    me = place_ref[0]
    first_col = 0
    for t in range(tiles):
        first_col = first_col + jnp.where(t < me, width_ref[t], 0)
    shift = first_col % (cols * pack)
    shift_blocks = shift // LANES
    shift_lanes = shift % LANES
    width = width_ref[me] - begin_row * cols - step * chunk

    @pl.when(step == 0)
    def _():
        lanes = pl.ds(begin_row // pack * LANES, here_scr.shape[2])
        copies = []
        for v, n in enumerate(parts):
            depth = here_scr.shape[1] // n
            for k in range(n):
                m = len(copies)
                target = here_scr.at[v, pl.ds(k * depth, depth), :]
                copies.append(pltpu.make_async_copy(x_refs[m].at[:, lanes], target, sem.at[m]))
                copies[-1].start()
        for copy in copies:
            copy.wait()

    spread = 0.0
    first = pl.multiple_of(step * (count * LANES), LANES)
    for v in range(len(parts)):
        spread = spread + jnp.dot(
            weight_ref[v],
            here_scr[v, :, pl.ds(first, (count + 1) * LANES)],
            preferred_element_type=jnp.float32,
        )
    for r in range(count + 1):
        for b in range(group):
            s_scr[:, pl.ds((r * group + b) * LANES, LANES)] = spread[
                b * levels : (b + 1) * levels, r * LANES : (r + 1) * LANES
            ]
    ordered = jnp.dot(order_ref[...], pert_ref[0], preferred_element_type=jnp.float32)
    lane = lax.broadcasted_iota(jnp.int32, (levels, LANES), 1)
    keep = lane < LANES - shift_lanes
    half = levels // 2

    def rolled(k):
        block = s_scr[:, pl.ds(pl.multiple_of((k + shift_blocks) * LANES, LANES), LANES)]
        return pltpu.roll(block, lax.rem(LANES - shift_lanes, LANES), 1)

    here = rolled(0)
    for k in range(count * group):
        after = rolled(k + 1)
        at = jnp.where(keep, here, after)
        part = pl.ds(k * LANES, LANES)
        value = ordered[:, k * LANES : (k + 1) * LANES] * at
        value = jnp.where(lane < width - k * LANES, value, 0.0).astype(jnp.bfloat16)
        own_ref[:, part] = value[:half]
        send_ref[:, part] = value[half:]
        here = after


def localize(begin_row, rows, cols, place, tile_widths, arrived, weight, order, perturbations):
    levels = perturbations.shape[1]
    chunk = ROWS_PER_BLOCK * cols
    assert rows % ROWS_PER_BLOCK == 0 and begin_row % ROWS_PER_BLOCK == 0
    skip = begin_row // ROWS_PER_BLOCK
    group = weight.shape[1] // levels
    parts = tuple(len(one) for one in arrived)
    scalars = pl.BlockSpec(memory_space=pltpu.SMEM)
    vector = pl.BlockSpec(memory_space=pltpu.VMEM)
    half = jax.ShapeDtypeStruct((levels // 2, rows * cols), jnp.bfloat16)
    half_spec = pl.BlockSpec((levels // 2, chunk), lambda i: (0, i))
    return pl.pallas_call(
        functools.partial(localize_kernel, begin_row, cols, parts),
        grid=(rows // ROWS_PER_BLOCK,),
        out_shape=(half, half),
        in_specs=[scalars] * 2 + [pl.BlockSpec(memory_space=pl.ANY)] * sum(parts) + [vector, vector,
                  pl.BlockSpec((1, levels, chunk), lambda i: (0, 0, i + skip))],
        out_specs=(half_spec, half_spec),
        scratch_shapes=[
            pltpu.VMEM((levels, chunk + group * LANES), jnp.float32),
            pltpu.VMEM(
                (len(parts), weight.shape[2], (rows // (group * LANES // cols) + 1) * LANES),
                jnp.bfloat16,
            ),
            pltpu.SemaphoreType.DMA((sum(parts),)),
        ],
        compiler_params=pltpu.CompilerParams(vmem_limit_bytes=16 << 20),
        name="localize",
    )(place, tile_widths, *sum(map(list, arrived), []), weight, order, perturbations)


def body(
    alpha_weights, perturbations, coef_x, coef_y, level_scale, level_map, tile_widths, band_widths
):
    _, lev_dev, _, cols = alpha_weights.shape
    _, levels, capacity = perturbations.shape
    tiles = tile_widths.shape[0]
    tall = capacity // cols
    assert sum(PIECES) == tall and lev_dev == 2
    groups = tiles // LINE
    mem = lax.axis_index("mem")
    place = lax.axis_index("lev").astype(jnp.int32).reshape(1)

    def shifted(dy, dz):
        return [
            (y * LINE + z, (y + dy) % groups * LINE + (z + dz) % LINE)
            for y in range(groups)
            for z in range(LINE)
        ]

    def smooth(v):
        return smooth_and_cut(
            v, place, level_scale, level_map, tile_widths, alpha_weights, coef_x, coef_y, tall
        )

    planes = smooth(0)
    come = [planes[0]]
    for d in range(1, LINE):
        come.append(lax.ppermute(planes[d], "lev", shifted(0, d)))
    outgoing = smooth(1)[0]
    arrived = lax.all_to_all(outgoing, "lev", split_axis=0, concat_axis=0, tiled=True)
    joined = []
    for e in range(groups):
        one = jnp.concatenate([plane[e] for plane in come], axis=0)
        if e > 0:
            one = lax.ppermute(one, "lev", shifted(e, 0))
        joined.append(one)
    inputs = (joined, [arrived.reshape(tiles * SUBS, -1)])

    slot = jnp.arange(levels)
    core = (mem + slot // 16) % CORES
    step = slot // 4 % RING
    ring = mem // CORES % RING ^ jnp.where(step == 3, 2, jnp.where(step == 0, 0, (step + core) % 2 * 2 + 1))
    half = (mem // (CORES * RING) + slot // 2) % HALVES
    row_level = half * 16 + ring * 4 + core * 2 + slot % 2
    order = (row_level[:, None] == slot[None, :]).astype(jnp.bfloat16)
    row_band = jnp.sum(jnp.where(row_level[:, None] == slot[None, :], band_widths[None, :], 0), 1)
    at = jnp.arange(tiles)
    near = (place[0] // LINE - at // LINE) % groups * LINE + (place[0] - at) % LINE
    col_slot = jnp.stack([near * lev_dev, at * lev_dev + 1])
    match = col_slot[:, :, None] == slot
    col_level = jnp.sum(jnp.where(match, level_map, 0), 2)
    match = col_level[:, :, None] == slot
    col_band = jnp.sum(jnp.where(match, band_widths, 0), 2)
    distance = jnp.abs(row_level[None, :, None] - col_level[:, None, :]).astype(jnp.float32)
    mutual = jnp.minimum(row_band[None, :, None], col_band[:, None, :]).astype(jnp.float32)
    local = jnp.where(distance <= mutual, jnp.exp(-distance * distance / (mutual * mutual)), 0.0)
    group = jnp.arange(SUBS)
    same = (group[:, None, None, None] == group).reshape(1, SUBS, 1, 1, SUBS)
    weight = jnp.where(same, local[:, None, :, :, None], 0.0).astype(jnp.bfloat16)
    weight = weight.reshape(lev_dev, SUBS * levels, tiles * SUBS)

    results = []
    begin = 0
    for rows_here in PIECES:
        own, other = localize(
            begin, rows_here, cols, place, tile_widths, inputs, weight, order, perturbations
        )
        results.append(sum_members(own, other))
        begin += rows_here
    return jnp.concatenate(results, axis=1)


def sum_members(own, other):
    def wide(x):
        return x.astype(jnp.float32)

    def narrow(x):
        return x.astype(jnp.bfloat16)

    def moved(dz, flips, dc):
        pairs = []
        for z in range(HALVES):
            for x in range(RING):
                for c in range(CORES):
                    to = ((z + dz) % HALVES, x ^ flips[c], (c + dc) % CORES)
                    pairs.append(((z * RING + x) * CORES + c, (to[0] * RING + to[1]) * CORES + to[2]))
        return pairs

    keep = own.shape[0] // 2
    came = lax.ppermute(other, "mem", moved(0, (0, 0), 1))
    mine = wide(own[:keep]) + wide(came[:keep])
    gone = narrow(wide(own[keep:]) + wide(came[keep:]))
    mine = mine + wide(lax.ppermute(gone, "mem", moved(0, (1, 3), 0)))
    keep //= 2
    beside = lax.ppermute(narrow(mine[keep:]), "mem", moved(0, (3, 1), 0))
    total = mine[:keep] + wide(beside)
    keep //= HALVES
    far = lax.ppermute(narrow(total[keep:]), "mem", moved(1, (0, 0), 0))
    return total[:keep] + wide(far)


def solution(mesh):
    placed = (P("mem", "lev", None, None), P("mem", None, "lev"), P(), P(), P(), P(), P(), P())

    return jax.shard_map(
        body, mesh=mesh, in_specs=placed, out_specs=P("mem", "lev"), check_vma=False
    )
```

```python
import functools

import jax
import jax.numpy as jnp
from jax import lax
from jax.experimental import pallas as pl
from jax.experimental.pallas import tpu as pltpu
from jax.sharding import PartitionSpec as P

STEPS = 16
LANES = 128
SUBS = 8
ROWS_PER_BLOCK = 8
CORES, RING, HALVES = 2, 4, 2
PIECES = (32, 16)
LINE = 4


def split_bf16(x):
    high = x.astype(jnp.bfloat16)
    return high, (x - high.astype(jnp.float32)).astype(jnp.bfloat16)


def diffuse_kernel(
    level, place_ref, scale_ref, map_ref, width_ref, alpha_ref, cx_ref, cy_ref, *refs
):
    out_refs = refs[:-15]
    (
        raw_scr, cx_scr, cy_scr, spread_scr, gather_scr, x_scr, f_scr, ax_scr, ay_scr, ayr_scr,
        o_scr, msg_scr, starts, sems, out_sem,
    ) = refs[-15:]
    rows, cols = cx_ref.shape
    levels = alpha_ref.shape[1]
    fold = rows // SUBS
    blocks = cols // LANES
    pack = SUBS // blocks
    tiles = width_ref.shape[0]

    def part(b):
        return pl.ds(b * LANES, LANES)

    def at(r):
        return pl.ds(r * SUBS, SUBS)

    sources = (cx_ref, cy_ref, alpha_ref.at[0, level])
    planes = (cx_scr, cy_scr, raw_scr)
    copies = [
        [
            pltpu.make_async_copy(source.at[:, part(b)], plane.at[b], sems.at[k, b])
            for b in range(blocks)
        ]
        for k, (source, plane) in enumerate(zip(sources, planes))
    ]
    for one in copies:
        for copy in one:
            copy.start()

    for b in range(blocks):
        natural = lax.broadcasted_iota(jnp.int32, (cols, LANES), 0)
        spaced = lax.broadcasted_iota(jnp.int32, (cols, LANES), 1)
        match = jnp.where(natural == spaced * blocks + b, 1.0, 0.0)
        spread_scr[:, part(b)] = match.astype(jnp.bfloat16)
        match = jnp.where(natural % LANES * blocks + natural // LANES == spaced + b * LANES, 1.0, 0.0)
        gather_scr[:, part(b)] = match.astype(jnp.bfloat16)

    def spread_columns(k):
        for copy in copies[k]:
            copy.wait()
        for r in range(fold):
            for b in range(blocks):
                x_scr[at(r), part(b)] = planes[k][b, pl.ds(r, SUBS, stride=fold), :]
        high, low = split_bf16(x_scr[...])
        return jnp.dot(high, spread_scr[...], preferred_element_type=jnp.float32) + jnp.dot(
            low, spread_scr[...], preferred_element_type=jnp.float32
        )

    lane = lax.broadcasted_iota(jnp.int32, (SUBS, LANES), 1)
    sub = lax.broadcasted_iota(jnp.int32, (SUBS, LANES), 0)
    gain = scale_ref[map_ref[place_ref[0] * levels + level]]
    ax_scr[...] = spread_columns(0) * gain
    ay_scr[...] = spread_columns(1) * gain
    for b in range(blocks):
        ax_scr[at(fold - 1), part(b)] = jnp.where(
            sub == SUBS - 1, 0.0, ax_scr[at(fold - 1), part(b)]
        )
    for r in range(fold):
        ay = jnp.where(lane == LANES - 1, 0.0, ay_scr[at(r), part(blocks - 1)])
        ay_scr[at(r), part(blocks - 1)] = ay
        ayr_scr[at(r), :] = pltpu.roll(ay, 1, 1)
    f_scr[pl.ds(0, rows), :] = spread_columns(2)

    @pl.loop(0, STEPS)
    def _(step):
        wrap = [pltpu.roll(f_scr[at(0), part(b)], SUBS - 1, 0) for b in range(blocks)]
        for b in range(blocks):
            f_scr[at(fold), part(b)] = wrap[b]
        here = [f_scr[at(fold - 1), part(b)] for b in range(blocks)]
        before = [
            pltpu.roll(ax_scr[at(fold - 1), part(b)] * (wrap[b] - here[b]), 1, 0)
            for b in range(blocks)
        ]
        here = [f_scr[at(0), part(b)] for b in range(blocks)]
        for r in range(fold):
            after = [f_scr[at(r + 1), part(b)] for b in range(blocks)]
            right = pltpu.roll(here[0], LANES - 1, 1)
            left = pltpu.roll(here[blocks - 1], 1, 1)
            last_y = ayr_scr[at(r), :] * (here[0] - left)
            flux = []
            for b in range(blocks):
                fx = ax_scr[at(r), part(b)] * (after[b] - here[b])
                beside = here[b + 1] if b < blocks - 1 else right
                fy = ay_scr[at(r), part(b)] * (beside - here[b])
                f_scr[at(r), part(b)] = here[b] + (fx - before[b]) + (fy - last_y)
                last_y = fy
                flux.append(fx)
            here, before = after, flux

    natural = jnp.dot(
        f_scr[pl.ds(0, rows), :].astype(jnp.bfloat16),
        gather_scr[...],
        preferred_element_type=jnp.float32,
    )
    for r in range(fold):
        for b in range(blocks):
            o_scr[at(r * blocks + b), :] = natural[
                r * SUBS : (r + 1) * SUBS, b * LANES : (b + 1) * LANES
            ]
    for r in range(fold // pack):
        for i in range(SUBS):
            row = o_scr[pl.ds(r * SUBS * SUBS + i, SUBS, stride=SUBS), :]
            msg_scr[:, part(i * (fold // pack) + r)] = row.astype(jnp.bfloat16)
    used = rows // pack * LANES
    msg_scr[:, pl.ds(used, msg_scr.shape[1] - used)] = jnp.zeros(
        (SUBS, msg_scr.shape[1] - used), jnp.bfloat16
    )
    first_col = 0
    for t in range(tiles):
        starts[t] = first_col
        first_col = first_col + width_ref[t]
    sends = []
    groups = tiles // LINE
    for k in range(tiles):
        d, e = k // groups, k % groups
        if len(out_refs) > 1:
            tile = lax.rem(place_ref[0] // LINE + e, groups) * LINE + lax.rem(place_ref[0] + d, LINE)
            target = out_refs[d].at[e]
        else:
            tile, target = k, out_refs[0].at[k]
        first = pl.multiple_of(starts[tile] // (cols * pack) * LANES, LANES)
        sends.append(
            pltpu.make_async_copy(
                msg_scr.at[:, pl.ds(first, out_refs[0].shape[2])], target, out_sem.at[k]
            )
        )
        sends[-1].start()
    for one in sends:
        one.wait()


def smooth_and_cut(level, place, level_scale, level_map, tile_widths, alpha, coef_x, coef_y, tall):
    rows, cols = alpha.shape[2:]
    tiles = tile_widths.shape[0]
    blocks = cols // LANES
    pack = SUBS // blocks
    assert SUBS % blocks == 0 and rows % (SUBS * pack) == 0
    anywhere = pl.BlockSpec(memory_space=pl.ANY)
    scalars = pl.BlockSpec(memory_space=pltpu.SMEM)
    plane = pltpu.VMEM((blocks, rows, LANES), jnp.float32)
    whole = pltpu.VMEM((rows, cols), jnp.float32)
    square = pltpu.VMEM((cols, cols), jnp.bfloat16)
    split = LINE if level == 0 else 1
    return pl.pallas_call(
        functools.partial(diffuse_kernel, level),
        out_shape=[
            jax.ShapeDtypeStruct((tiles // split, SUBS, (tall // pack + 1) * LANES), jnp.bfloat16)
        ]
        * split,
        in_specs=[scalars] * 4 + [anywhere] * 3,
        out_specs=[anywhere] * split,
        scratch_shapes=[
            plane,
            plane,
            plane,
            square,
            square,
            whole,
            pltpu.VMEM((rows + SUBS, cols), jnp.float32),
            whole,
            whole,
            pltpu.VMEM((rows, LANES), jnp.float32),
            pltpu.VMEM((rows * blocks, LANES), jnp.float32),
            pltpu.VMEM((SUBS, ((rows + tall) // pack + 1) * LANES), jnp.bfloat16),
            pltpu.SMEM((tiles,), jnp.int32),
            pltpu.SemaphoreType.DMA((3, blocks)),
            pltpu.SemaphoreType.DMA((tiles,)),
        ],
        name="diffuse",
    )(place, level_scale, level_map, tile_widths, alpha, coef_x, coef_y)


def reorder_kernel(order_ref, pert_ref, out_ref):
    rows = jnp.dot(order_ref[...], pert_ref[0], preferred_element_type=jnp.float32)
    out_ref[...] = rows.astype(out_ref.dtype)


def reorder(order, perturbations):
    _, levels, capacity = perturbations.shape
    chunk = capacity // 6
    return pl.pallas_call(
        reorder_kernel,
        grid=(capacity // chunk,),
        out_shape=jax.ShapeDtypeStruct((levels, capacity), perturbations.dtype),
        in_specs=[
            pl.BlockSpec(memory_space=pltpu.VMEM),
            pl.BlockSpec((1, levels, chunk), lambda i: (0, 0, i)),
        ],
        out_specs=pl.BlockSpec((levels, chunk), lambda i: (0, i)),
        compiler_params=pltpu.CompilerParams(vmem_limit_bytes=8 << 20),
        name="reorder",
    )(order, perturbations)


def localize_kernel(
    begin_row, cols, parts, place_ref, width_ref, *refs
):
    x_refs = refs[: sum(parts)]
    weight_ref, pert_ref, own_ref, send_ref, s_scr, here_scr, sem = refs[sum(parts) :]
    step = pl.program_id(0)
    tiles = width_ref.shape[0]
    levels = pert_ref.shape[0]
    blocks = cols // LANES
    group = weight_ref.shape[1] // levels
    pack = group // blocks
    chunk = pert_ref.shape[1]
    count = chunk // (cols * pack)
    me = place_ref[0]
    first_col = 0
    for t in range(tiles):
        first_col = first_col + jnp.where(t < me, width_ref[t], 0)
    shift = first_col % (cols * pack)
    shift_blocks = shift // LANES
    shift_lanes = shift % LANES
    width = width_ref[me] - begin_row * cols - step * chunk

    @pl.when(step == 0)
    def _():
        lanes = pl.ds(begin_row // pack * LANES, here_scr.shape[2])
        copies = []
        for v, n in enumerate(parts):
            depth = here_scr.shape[1] // n
            for k in range(n):
                m = len(copies)
                target = here_scr.at[v, pl.ds(k * depth, depth), :]
                copies.append(pltpu.make_async_copy(x_refs[m].at[:, lanes], target, sem.at[m]))
                copies[-1].start()
        for copy in copies:
            copy.wait()

    spread = 0.0
    first = pl.multiple_of(step * (count * LANES), LANES)
    for v in range(len(parts)):
        spread = spread + jnp.dot(
            weight_ref[v],
            here_scr[v, :, pl.ds(first, (count + 1) * LANES)],
            preferred_element_type=jnp.float32,
        )
    for r in range(count + 1):
        for b in range(group):
            s_scr[:, pl.ds((r * group + b) * LANES, LANES)] = spread[
                b * levels : (b + 1) * levels, r * LANES : (r + 1) * LANES
            ]
    ordered = pert_ref[...].astype(jnp.float32)
    lane = lax.broadcasted_iota(jnp.int32, (levels, LANES), 1)
    keep = lane < LANES - shift_lanes
    half = levels // 2

    def rolled(k):
        block = s_scr[:, pl.ds(pl.multiple_of((k + shift_blocks) * LANES, LANES), LANES)]
        return pltpu.roll(block, lax.rem(LANES - shift_lanes, LANES), 1)

    here = rolled(0)
    for k in range(count * group):
        after = rolled(k + 1)
        at = jnp.where(keep, here, after)
        part = pl.ds(k * LANES, LANES)
        value = ordered[:, k * LANES : (k + 1) * LANES] * at
        value = jnp.where(lane < width - k * LANES, value, 0.0).astype(jnp.bfloat16)
        own_ref[:, part] = value[:half]
        send_ref[:, part] = value[half:]
        here = after


def localize(begin_row, rows, cols, place, tile_widths, arrived, weight, ordered):
    levels = ordered.shape[0]
    chunk = ROWS_PER_BLOCK * cols
    assert rows % ROWS_PER_BLOCK == 0 and begin_row % ROWS_PER_BLOCK == 0
    skip = begin_row // ROWS_PER_BLOCK
    group = weight.shape[1] // levels
    parts = tuple(len(one) for one in arrived)
    scalars = pl.BlockSpec(memory_space=pltpu.SMEM)
    vector = pl.BlockSpec(memory_space=pltpu.VMEM)
    half = jax.ShapeDtypeStruct((levels // 2, rows * cols), jnp.bfloat16)
    half_spec = pl.BlockSpec((levels // 2, chunk), lambda i: (0, i))
    return pl.pallas_call(
        functools.partial(localize_kernel, begin_row, cols, parts),
        grid=(rows // ROWS_PER_BLOCK,),
        out_shape=(half, half),
        in_specs=[scalars] * 2 + [pl.BlockSpec(memory_space=pl.ANY)] * sum(parts)
        + [vector, pl.BlockSpec((levels, chunk), lambda i: (0, i + skip))],
        out_specs=(half_spec, half_spec),
        scratch_shapes=[
            pltpu.VMEM((levels, chunk + group * LANES), jnp.float32),
            pltpu.VMEM(
                (len(parts), weight.shape[2], (rows // (group * LANES // cols) + 1) * LANES),
                jnp.bfloat16,
            ),
            pltpu.SemaphoreType.DMA((sum(parts),)),
        ],
        compiler_params=pltpu.CompilerParams(vmem_limit_bytes=8 << 20),
        name="localize",
    )(place, tile_widths, *sum(map(list, arrived), []), weight, ordered)


def body(
    alpha_weights, perturbations, coef_x, coef_y, level_scale, level_map, tile_widths, band_widths
):
    _, lev_dev, _, cols = alpha_weights.shape
    _, levels, capacity = perturbations.shape
    tiles = tile_widths.shape[0]
    tall = capacity // cols
    assert sum(PIECES) == tall and lev_dev == 2
    groups = tiles // LINE
    mem = lax.axis_index("mem")
    place = lax.axis_index("lev").astype(jnp.int32).reshape(1)

    def shifted(dy, dz):
        return [
            (y * LINE + z, (y + dy) % groups * LINE + (z + dz) % LINE)
            for y in range(groups)
            for z in range(LINE)
        ]

    def smooth(v):
        return smooth_and_cut(
            v, place, level_scale, level_map, tile_widths, alpha_weights, coef_x, coef_y, tall
        )

    planes = smooth(0)
    come = [planes[0]]
    for d in range(1, LINE):
        come.append(lax.ppermute(planes[d], "lev", shifted(0, d)))
    outgoing = smooth(1)[0]
    arrived = lax.all_to_all(outgoing, "lev", split_axis=0, concat_axis=0, tiled=True)
    joined = []
    for e in range(groups):
        one = jnp.concatenate([plane[e] for plane in come], axis=0)
        if e > 0:
            one = lax.ppermute(one, "lev", shifted(e, 0))
        joined.append(one)
    inputs = (joined, [arrived.reshape(tiles * SUBS, -1)])

    slot = jnp.arange(levels)
    core = (mem + slot // 16) % CORES
    step = slot // 4 % RING
    ring = mem // CORES % RING ^ jnp.where(step == 3, 2, jnp.where(step == 0, 0, (step + core) % 2 * 2 + 1))
    half = (mem // (CORES * RING) + slot // 2) % HALVES
    row_level = half * 16 + ring * 4 + core * 2 + slot % 2
    order = (row_level[:, None] == slot[None, :]).astype(jnp.bfloat16)
    ordered = reorder(order, perturbations)
    row_band = jnp.sum(jnp.where(row_level[:, None] == slot[None, :], band_widths[None, :], 0), 1)
    at = jnp.arange(tiles)
    near = (place[0] // LINE - at // LINE) % groups * LINE + (place[0] - at) % LINE
    col_slot = jnp.stack([near * lev_dev, at * lev_dev + 1])
    match = col_slot[:, :, None] == slot
    col_level = jnp.sum(jnp.where(match, level_map, 0), 2)
    match = col_level[:, :, None] == slot
    col_band = jnp.sum(jnp.where(match, band_widths, 0), 2)
    distance = jnp.abs(row_level[None, :, None] - col_level[:, None, :]).astype(jnp.float32)
    mutual = jnp.minimum(row_band[None, :, None], col_band[:, None, :]).astype(jnp.float32)
    local = jnp.where(distance <= mutual, jnp.exp(-distance * distance / (mutual * mutual)), 0.0)
    group = jnp.arange(SUBS)
    same = (group[:, None, None, None] == group).reshape(1, SUBS, 1, 1, SUBS)
    weight = jnp.where(same, local[:, None, :, :, None], 0.0).astype(jnp.bfloat16)
    weight = weight.reshape(lev_dev, SUBS * levels, tiles * SUBS)

    results = []
    begin = 0
    for rows_here in PIECES:
        own, other = localize(begin, rows_here, cols, place, tile_widths, inputs, weight, ordered)
        results.append(sum_members(own, other))
        begin += rows_here
    return jnp.concatenate(results, axis=1)


def sum_members(own, other):
    def wide(x):
        return x.astype(jnp.float32)

    def narrow(x):
        return x.astype(jnp.bfloat16)

    def moved(dz, flips, dc):
        pairs = []
        for z in range(HALVES):
            for x in range(RING):
                for c in range(CORES):
                    to = ((z + dz) % HALVES, x ^ flips[c], (c + dc) % CORES)
                    pairs.append(((z * RING + x) * CORES + c, (to[0] * RING + to[1]) * CORES + to[2]))
        return pairs

    keep = own.shape[0] // 2
    came = lax.ppermute(other, "mem", moved(0, (0, 0), 1))
    mine = wide(own[:keep]) + wide(came[:keep])
    gone = narrow(wide(own[keep:]) + wide(came[keep:]))
    got = lax.ppermute(gone, "mem", moved(0, (1, 3), 0))
    mine = mine + wide(got)
    keep //= 2
    narrowed = narrow(mine[keep:])
    beside = lax.ppermute(narrowed, "mem", moved(0, (3, 1), 0))
    total = mine[:keep] + wide(beside)
    keep //= HALVES
    narrowed = narrow(total[keep:])
    far = lax.ppermute(narrowed, "mem", moved(1, (0, 0), 0))
    return total[:keep] + wide(far)


def solution(mesh):
    placed = (P("mem", "lev", None, None), P("mem", None, "lev"), P(), P(), P(), P(), P(), P())

    return jax.shard_map(
        body, mesh=mesh, in_specs=placed, out_specs=P("mem", "lev"), check_vma=False
    )
```
